512 devices in a mesh: tx: 32 (over y, z_lo, core), ty: 16 (over z_hi, x).
Axes of the slice: x: 4, y: 8, z: 8 (z_hi: 4, z_lo: 2; z = z_hi * 2 + z_lo), core: 2. Of those that a mesh axis runs over, the one named last changes fastest.
Arguments:
- offsets: float32 [2, 64, 64, 128], P(None, 'tx', 'ty'), may hold values from 0 to 1
- circ: float32 [64, 64, 128], P('tx', 'ty'), as said below
- counts: int32 [64, 64], P('tx', 'ty'), may hold values from 1 to 128, as said below
Outputs:
- velocity: float32 [2, 64, 64, 128], P(None, 'tx', 'ty')
- moved: float32 [2, 64, 64, 128], P(None, 'tx', 'ty')
The draws below stay inside these ranges and needn't reach their ends.
Inputs may be any that keep to these rules, and one draw needn't show every extreme that they name: counts of live slots in each cell; at least one cell holds 128; the middle quarter of the cell rows holds more on average. `circ`: circulations of order 0.02 / sqrt(128), of both signs.
All inputs are finite; a program needn't handle non-finite values.
Results may differ from the reference program's by a relative error of at most 0.00011.
Values sent between devices are 32-bit elements; how exact they have to be, the bound alone decides.
A program may use at most 64 MiB of HBM per device.

```python
import math
import jax
import jax.numpy as jnp
from jax import lax

MODES = 64
P_SIZE = 128
NCELL = 64


def draw_counts(key, part):
    first_key, second = jax.random.split(jax.random.fold_in(key, 11))
    base_count = jax.random.randint(first_key, (NCELL, NCELL), 1, P_SIZE + 1)
    extra_count = jax.random.randint(second, (NCELL, NCELL), 1, P_SIZE + 1)
    row_index = jnp.arange(NCELL, dtype=jnp.int32)[:, None]
    in_band = (row_index >= 3 * NCELL // 8) & (row_index < 5 * NCELL // 8)
    counts = jnp.where(in_band, jnp.maximum(base_count, extra_count), base_count)
    return counts.at[0, 0].set(P_SIZE).astype(jnp.int32)


def draw_circ(key, part):
    first_key, second = jax.random.split(jax.random.fold_in(key, 23))
    rough_part = jnp.clip(jax.random.normal(first_key, (NCELL, NCELL, P_SIZE), jnp.float32), -5.0, 5.0)
    spread = jnp.exp(jax.random.uniform(second, (NCELL, NCELL, P_SIZE), jnp.float32, -1.15, 1.15))
    scale_factor = 0.014 / math.sqrt(P_SIZE)
    return scale_factor * rough_part * spread


def shard_levels(own_key, shape, pieces, least, high):
    factor_of = 1.0
    for axis_at, parts in pieces:
        heights = jax.random.uniform(jax.random.fold_in(jax.random.fold_in(own_key, 6), axis_at), (parts,), jnp.float32, least / len(pieces), high / len(pieces))
        factor_of = factor_of * jnp.repeat(jnp.exp(heights), shape[axis_at] // parts).reshape((-1,) + (1,) * (len(shape) - 1 - axis_at))
    return factor_of


def setup_inputs(seed: int = 0) -> dict:
    key_list = jax.random.split(jax.random.key(seed), 4)
    offsets = jnp.clip(1.0 * jax.random.uniform(key_list[0], (2, NCELL, NCELL, P_SIZE), jnp.float32) ** shard_levels(key_list[0], (2, NCELL, NCELL, P_SIZE), ((1, 32), (2, 16)), -0.2, 0.2), 0.0, 1.0)
    circ = draw_circ(jax.random.fold_in(key_list[3], 71), 0)
    counts = draw_counts(jax.random.fold_in(key_list[3], 71), 0)
    return dict(offsets=offsets, circ=circ, counts=counts)


two_pi = 2.0 * math.pi
screen = 1.5625
smooth = 0.0625
section_step = 0.25


def pair_sum(target, source, shift_rows, shift_cols):
    offset_x = target[0][:, :, None] - source[0][:, None, :] - shift_cols
    offset_y = target[1][:, :, None] - source[1][:, None, :] - shift_rows
    square = offset_x * offset_x + offset_y * offset_y
    weight = source[2][:, None, :] * jnp.exp(-screen * square) / (square + smooth)
    return jnp.stack([jnp.sum(-offset_y * weight, axis=2), jnp.sum(offset_x * weight, axis=2)])


def near_row(window):
    span_cols = window.shape[2] - 2
    target = window[:, 1, 1:1 + span_cols]
    summed = jnp.zeros((2,) + target.shape[1:], jnp.float32)
    for shift_rows in (-1, 0, 1):
        for shift_cols in (-1, 0, 1):
            source = window[:, 1 + shift_rows, 1 + shift_cols:1 + shift_cols + span_cols]
            summed = summed + pair_sum(target, source, float(shift_rows), float(shift_cols))
    return summed


def wave_numbers():
    return (jnp.arange(MODES, dtype=jnp.int32) - MODES // 2).astype(jnp.float32)


def mode_grid(cell_count):
    wave_number = wave_numbers()
    wave_x = two_pi * wave_number[:, None] * jnp.ones((1, MODES), jnp.float32)
    wave_y = two_pi * wave_number[None, :] * jnp.ones((MODES, 1), jnp.float32)
    square = wave_x * wave_x + wave_y * wave_y
    edge_mode = wave_number == -(MODES // 2)
    zero_mode = wave_number == 0
    keep_mode = jnp.logical_not(edge_mode[:, None] | edge_mode[None, :] | (zero_mode[:, None] & zero_mode[None, :]))
    safe_square = jnp.where(keep_mode, square, 1.0)
    damping = jnp.where(keep_mode, jnp.exp(-safe_square / (6.25 * cell_count * cell_count)) / safe_square, 0.0)
    return damping, wave_x, wave_y


def tables(coord):
    phase_angle = two_pi * wave_numbers()[:, None] * coord[None, :]
    return jnp.cos(phase_angle), jnp.sin(phase_angle)


def contract(left_side, right_side):
    return lax.dot_general(left_side, right_side, (((1,), (1,)), ((), ())), precision=lax.Precision.HIGHEST, preferred_element_type=jnp.float32)


def product(left_side, right_side):
    return jnp.dot(left_side, right_side, precision=lax.Precision.HIGHEST, preferred_element_type=jnp.float32)


def structure(x_position, y_position, strength):
    cos_x, sin_x = tables(x_position)
    cos_y, sin_y = tables(y_position)
    real_part = contract(strength * cos_x, cos_y) - contract(strength * sin_x, sin_y)
    imag_part = contract(strength * sin_x, cos_y) + contract(strength * cos_x, sin_y)
    return jnp.stack([real_part, imag_part])


def far_velocity(x_position, y_position, scaled, wave_x, wave_y):
    cos_x, sin_x = tables(x_position)
    cos_y, sin_y = tables(y_position)
    with_imag = jnp.concatenate([wave_y * scaled[1], -wave_x * scaled[1]])
    with_real = jnp.concatenate([wave_y * scaled[0], -wave_x * scaled[0]])
    term_cos = (product(with_imag, cos_y) - product(with_real, sin_y)).reshape(2, MODES, -1)
    term_sin = (product(with_real, cos_y) + product(with_imag, sin_y)).reshape(2, MODES, -1)
    return jnp.sum(cos_x[None] * term_cos - sin_x[None] * term_sin, axis=1)


def reference(offsets, circ, counts):
    live_slot = jnp.arange(P_SIZE, dtype=jnp.int32)[None, None, :] < counts[:, :, None]
    strength = jnp.where(live_slot, circ, 0.0)
    packed = jnp.stack([offsets[0], offsets[1], strength])
    padded = jnp.pad(packed, ((0, 0), (1, 1), (1, 1), (0, 0)), mode="wrap")
    near_part = lax.map(lambda first_row: near_row(lax.dynamic_slice_in_dim(padded, first_row, 3, 1)), jnp.arange(NCELL, dtype=jnp.int32))
    near_part = jnp.transpose(near_part, (1, 0, 2, 3)) * (NCELL / two_pi)
    cell_pos = jnp.arange(NCELL, dtype=jnp.int32).astype(jnp.float32)
    x_position = (cell_pos[None, :, None] + offsets[0]) / NCELL
    y_position = (cell_pos[:, None, None] + offsets[1]) / NCELL

    def row_modes(row_index):
        return structure(x_position[row_index].reshape(-1), y_position[row_index].reshape(-1), strength[row_index].reshape(-1))

    partial_modes = lax.map(row_modes, jnp.arange(NCELL, dtype=jnp.int32))
    summed = jnp.sum(partial_modes, axis=0)
    damping, wave_x, wave_y = mode_grid(NCELL)
    scaled = damping[None] * summed

    def row_far(row_index):
        return far_velocity(x_position[row_index].reshape(-1), y_position[row_index].reshape(-1), scaled, wave_x, wave_y).reshape(2, NCELL, P_SIZE)

    far_part = lax.map(row_far, jnp.arange(NCELL, dtype=jnp.int32))
    far_part = jnp.transpose(far_part, (1, 0, 2, 3))
    velocity = jnp.where(live_slot[None], near_part + far_part, 0.0)
    moved = offsets + section_step * velocity
    return velocity, moved
```

```python
import math

import jax
import jax.numpy as jnp
from jax import lax
from jax.experimental import pallas as pl
from jax.experimental.pallas import tpu as pltpu
from jax.sharding import PartitionSpec as P

MESH = pl.DeviceIdType.MESH
CELLS = 64
HALF = 32
ROWS, COLS = 2, 4
TILE = ROWS * COLS
SLOTS = 128
NX, NY, NZ = 4, 8, 8
TX, TY = 32, 16

two_pi = 2.0 * math.pi
screen = 1.5625
smooth = 0.0625
section_step = 0.25
alpha = screen / math.log(2.0)
sigma = math.sqrt(alpha)
near_scale = CELLS / two_pi * sigma
directions = tuple((dr, dc) for dr in (-1, 0, 1) for dc in (-1, 0, 1) if (dr, dc) != (0, 0))


def mesh_id(x, y, z, c):
    return (y * 4 + lax.rem(z, 2) * 2 + c, lax.div(z, 2) * 4 + x)


def fan(tx, ty):
    return (
        lax.rem(ty, 4),
        lax.div(tx, 4),
        lax.div(ty, 4) * 2 + lax.rem(lax.div(tx, 2), 2),
        lax.rem(tx, 2),
    )


def cos_sin(turns):
    rest = turns - jnp.round(turns)
    half = rest * math.pi
    z = half * half
    sine = half * (
        1.0
        + z
        * (
            -1.0 / 6
            + z * (1.0 / 120 + z * (-1.0 / 5040 + z * (1.0 / 362880 + z * (-1.0 / 39916800))))
        )
    )
    cosine = 1.0 + z * (
        -0.5
        + z
        * (
            1.0 / 24
            + z
            * (-1.0 / 720 + z * (1.0 / 40320 + z * (-1.0 / 3628800 + z * (1.0 / 479001600))))
        )
    )
    return 1.0 - 2.0 * sine * sine, 2.0 * sine * cosine


def split(value):
    high = value.astype(jnp.bfloat16)
    return high, (value - high.astype(jnp.float32)).astype(jnp.bfloat16)


def mode_factors():
    lane = lax.broadcasted_iota(jnp.int32, (HALF, 128), 1)
    row = lax.broadcasted_iota(jnp.int32, (HALF, 128), 0)
    wave_n = lax.rem(lane, HALF)
    k_x = two_pi * row.astype(jnp.float32)
    k_y = two_pi * wave_n.astype(jnp.float32)
    square = k_x * k_x + k_y * k_y
    keep = jnp.logical_or(row > 0, wave_n > 0)
    safe = jnp.where(keep, square, 1.0)
    damping = jnp.where(keep, jnp.exp(safe * (-1.0 / (6.25 * CELLS * CELLS))) / safe, 0.0)
    images = jnp.where(row > 0, 2.0, 1.0) * jnp.where(wave_n > 0, 2.0, 1.0)
    damping = damping * images
    for_u = damping * k_y * jnp.where(lax.rem(lane, 64) < HALF, 1.0, -1.0)
    for_v = damping * k_x * jnp.where(lane < 64, 1.0, -1.0)
    return for_u, for_v


def halo_box(dr, dc):
    src_rows = {-1: (1, 1), 0: (1, ROWS), 1: (ROWS, 1)}[dr]
    src_cols = {-1: (1, 1), 0: (1, COLS), 1: (COLS, 1)}[dc]
    dst_rows = {-1: (ROWS + 1, 1), 0: (1, ROWS), 1: (0, 1)}[dr]
    dst_cols = {-1: (COLS + 1, 1), 0: (1, COLS), 1: (0, 1)}[dc]
    return tuple(pl.ds(*a) for a in (src_rows, src_cols, dst_rows, dst_cols))


def near_targets(row, col):
    return [
        r * COLS + c
        for r in range(ROWS)
        for c in range(COLS)
        if abs(row - 1 - r) <= 1 and abs(col - 1 - c) <= 1
    ]


def add_near(sources, target, total, cells):
    for at_x, at_y, at_s, targets in cells:
        target_x = [jnp.broadcast_to(target[t : t + 1, :], (8, SLOTS)) for t in targets]
        target_y = [
            jnp.broadcast_to(target[TILE + t : TILE + t + 1, :], (8, SLOTS)) for t in targets
        ]

        def group(g, sums, at_x=at_x, at_y=at_y, at_s=at_s, tx=target_x, ty=target_y):
            rows = pl.ds(pl.multiple_of(g * 8, 8), 8)
            source_x = jnp.broadcast_to(sources[rows, at_x : at_x + 1], (8, SLOTS))
            source_y = jnp.broadcast_to(sources[rows, at_y : at_y + 1], (8, SLOTS))
            strength = jnp.broadcast_to(sources[rows, at_s : at_s + 1], (8, SLOTS))
            out = []
            for k in range(len(tx)):
                a = tx[k] - source_x
                b = ty[k] - source_y
                q = a * a + b * b
                w = strength / (jnp.exp2(q) * (q + smooth * alpha))
                out.append(sums[2 * k] - b * w)
                out.append(sums[2 * k + 1] + a * w)
            return tuple(out)

        start = tuple(total[2 * t + i] for t in targets for i in range(2))
        sums = lax.fori_loop(0, SLOTS // 8, group, start)
        for k, t in enumerate(targets):
            total[2 * t] = sums[2 * k]
            total[2 * t + 1] = sums[2 * k + 1]


def kernel(
    off, circ, counts, velocity, moved,
    ext, own_rows, own_t, halo_rows, halo_t, total, near_uv, tab_x, tab_y, sided, factors,
    part, z_buf, y_buf, x_buf, final,
    halo_send, halo_recv, half_send, z_recv, y_send, y_recv, x_send, x_recv, down_send, down_recv,
    go,
):
    tx, ty = lax.axis_index("tx"), lax.axis_index("ty")
    x, y, z, c = fan(tx, ty)
    is_root = z == 0
    barrier = pltpu.get_barrier_semaphore()

    def greet(device):
        pl.semaphore_signal(barrier, inc=1, device_id=device, device_id_type=MESH)

    def copy(src, dst, send, recv, device):
        return pltpu.make_async_remote_copy(
            src_ref=src, dst_ref=dst, send_sem=send, recv_sem=recv,
            device_id=device, device_id_type=MESH,
        )

    neighbours = []
    for dr, dc in directions:
        n_tx, n_ty = lax.rem(tx + (TX + dr), TX), lax.rem(ty + (TY + dc), TY)
        neighbours.append((n_tx, n_ty))
        n_x, n_y, _, n_c = fan(n_tx, n_ty)
        greet(mesh_id(n_x, n_y, 0, n_c))

    @pl.when(jnp.logical_not(is_root))
    def _():
        greet(mesh_id(x, y, 0, c))

    @pl.when(is_root)
    def _():
        for up in range(NZ - 1, 0, -1):
            for core in range(2):
                greet(mesh_id(x, y, up, core))
        for k in range(1, NY):
            greet(mesh_id(x, lax.rem(y + k, NY), 0, c))
        for k in range(1, 2 * NX):
            greet(mesh_id(lax.rem(x + k // 2, NX), y, 0, lax.rem(c + k, 2)))

    row_of = lax.broadcasted_iota(jnp.int32, (TILE, SLOTS), 0)
    lane_of = lax.broadcasted_iota(jnp.int32, (TILE, SLOTS), 1)
    count = jnp.zeros((TILE, SLOTS), jnp.int32)
    for cell in range(TILE):
        count = jnp.where(row_of == cell, counts[cell], count)
    live = lane_of < count
    off_x, off_y = off[0], off[1]
    strength = jnp.where(live, circ[...], 0.0)
    cell_row = lax.div(row_of, COLS).astype(jnp.float32)
    cell_col = lax.rem(row_of, COLS).astype(jnp.float32)
    own_rows[2 * TILE : 3 * TILE, :] = strength

    wave = lax.broadcasted_iota(jnp.int32, (HALF, SLOTS), 0).astype(jnp.float32)
    first_col = (ty * COLS).astype(jnp.float32)
    first_row = (tx * ROWS).astype(jnp.float32)
    for cell in range(TILE):
        lanes = slice(cell * SLOTS, (cell + 1) * SLOTS)
        pos_x = (off[0, cell : cell + 1, :] + (first_col + cell % COLS)) * (1.0 / CELLS)
        pos_y = (off[1, cell : cell + 1, :] + (first_row + cell // COLS)) * (1.0 / CELLS)
        weight = own_rows[2 * TILE + cell : 2 * TILE + cell + 1, :]
        for at, table in enumerate(cos_sin(wave * pos_x)):
            rows = slice(at * HALF, (at + 1) * HALF)
            tab_x[rows, lanes] = table
            high, low = split(table * weight)
            sided[rows, lanes] = high
            sided[64 + at * HALF : 64 + (at + 1) * HALF, lanes] = low
        for at, table in enumerate(cos_sin(wave * pos_y)):
            high, low = split(table)
            tab_y[at * HALF : (at + 1) * HALF, lanes] = high
            tab_y[64 + at * HALF : 64 + (at + 1) * HALF, lanes] = high
            tab_y[128 + at * HALF : 128 + (at + 1) * HALF, lanes] = low
    sums = lax.dot_general(
        sided[...], tab_y[64:192, :], (((1,), (1,)), ((), ())),
        preferred_element_type=jnp.float32,
    )
    sums = sums[0:64] + sums[64:128]
    sums = sums + pltpu.roll(sums, 64, 1)
    wide = lax.broadcasted_iota(jnp.int32, (HALF, 128), 1)
    packed = jnp.where(wide < 64, sums[0:HALF], sums[HALF:64])
    part[0] = packed[0:16]
    part[1] = packed[16:32]

    def half_copy(h):
        return copy(
            part.at[h], z_buf.at[z * 2 + c], half_send.at[h], z_recv.at[z * 2 + c],
            mesh_id(x, y, 0, h),
        )

    @pl.when(jnp.logical_not(is_root))
    def _():
        pl.semaphore_wait(barrier, 2)
        for h in range(2):
            half_copy(h).start()

    for cell in range(TILE):
        ext[1 + cell // COLS, 1 + cell % COLS, 0] = off[0, cell : cell + 1, :]
        ext[1 + cell // COLS, 1 + cell % COLS, 1] = off[1, cell : cell + 1, :]
        ext[1 + cell // COLS, 1 + cell % COLS, 2] = own_rows[
            2 * TILE + cell : 2 * TILE + cell + 1, :
        ]
    own_rows[0:TILE, :] = (off_x + cell_col) * sigma
    own_rows[TILE : 2 * TILE, :] = (off_y + cell_row) * sigma
    own_t[...] = jnp.transpose(own_rows[...])
    total[...] = jnp.zeros_like(total)
    for_u, for_v = mode_factors()
    factors[0] = for_u
    factors[1] = for_v
    add_near(
        own_t, own_rows, total,
        [
            (k, TILE + k, 2 * TILE + k, near_targets(1 + k // COLS, 1 + k % COLS))
            for k in range(TILE)
        ],
    )

    other = 1 - c
    mate = copy(
        part.at[other], z_buf.at[c], half_send.at[0], z_recv.at[c], mesh_id(x, y, 0, other)
    )

    @pl.when(is_root)
    def _():
        pl.semaphore_wait(barrier, 64 + (NZ - 1) + (NY - 1) + (2 * NX - 1))
        mate.start()
        for up in range(1, NZ):
            pl.semaphore_signal(
                go, inc=1, device_id=mesh_id(x, y, up, c), device_id_type=MESH
            )

    @pl.when(jnp.logical_not(is_root))
    def _():
        pl.semaphore_wait(go, 1)

    halo = []
    for k, (dr, dc) in enumerate(directions):
        src_rows, src_cols, dst_rows, dst_cols = halo_box(dr, dc)
        halo.append(
            copy(
                ext.at[src_rows, src_cols], ext.at[dst_rows, dst_cols],
                halo_send.at[k], halo_recv.at[k], neighbours[k],
            )
        )
        halo[-1].start()

    y_copies = [
        copy(
            y_buf.at[y], y_buf.at[y], y_send.at[k], y_recv.at[y],
            mesh_id(x, lax.rem(y + k, NY), 0, c),
        )
        for k in range(1, NY)
    ]
    x_copies = [
        copy(
            x_buf.at[c * NX + x], x_buf.at[c * NX + x], x_send.at[k], x_recv.at[c * NX + x],
            mesh_id(lax.rem(x + k // 2, NX), y, 0, lax.rem(c + k, 2)),
        )
        for k in range(1, 2 * NX)
    ]
    down_copies = [
        copy(final, final, down_send.at[k], down_recv, mesh_id(x, y, k, c)) for k in range(1, NZ)
    ]

    @pl.when(is_root)
    def _():
        z_buf[c] = part[c]
        for up in range(1, NZ):
            for core in range(2):
                slot = up * 2 + core
                copy(part.at[0], z_buf.at[slot], half_send.at[0], z_recv.at[slot], (tx, ty)).wait_recv()
        copy(part.at[0], z_buf.at[other], half_send.at[0], z_recv.at[other], (tx, ty)).wait_recv()
        y_buf[y] = jnp.sum(z_buf[...], axis=0)
        for k in (4, 3, 5, 2, 6, 1, 7):
            y_copies[k - 1].start()
        for k in range(1, NY):
            slot = lax.rem(y + k, NY)
            copy(part.at[0], y_buf.at[slot], y_send.at[0], y_recv.at[slot], (tx, ty)).wait_recv()
        x_buf[c * NX + x] = jnp.sum(y_buf[...], axis=0)
        for k in (4, 5, 2, 3, 6, 7, 1):
            x_copies[k - 1].start()

    border = [
        (r, q) for r in range(ROWS + 2) for q in range(COLS + 2)
        if r in (0, ROWS + 1) or q in (0, COLS + 1)
    ]
    for sent in halo:
        sent.wait_recv()
    for k, (r, q) in enumerate(border):
        halo_rows[k : k + 1, :] = (ext[r, q, 0] + (q - 1.0)) * sigma
        halo_rows[16 + k : 17 + k, :] = (ext[r, q, 1] + (r - 1.0)) * sigma
        halo_rows[32 + k : 33 + k, :] = ext[r, q, 2]
    halo_t[...] = jnp.transpose(halo_rows[...])
    add_near(
        halo_t, own_rows, total,
        [(k, 16 + k, 32 + k, near_targets(r, q)) for k, (r, q) in enumerate(border)],
    )
    for t in range(TILE):
        for i in range(2):
            near_uv[i, t : t + 1, :] = jnp.sum(total[2 * t + i], axis=0, keepdims=True) * near_scale

    @pl.when(is_root)
    def _():
        for k in range(1, 2 * NX):
            slot = lax.rem(c + k, 2) * NX + lax.rem(x + k // 2, NX)
            copy(part.at[0], x_buf.at[slot], x_send.at[0], x_recv.at[slot], (tx, ty)).wait_recv()
        for h in range(2):
            final[h] = jnp.sum(x_buf[h * NX : (h + 1) * NX], axis=0)
        for k in range(1, NZ):
            down_copies[k - 1].start()

    @pl.when(jnp.logical_not(is_root))
    def _():
        down_copies[0].wait_recv()

    modes = jnp.concatenate([final[0], final[1]], axis=0)
    swapped = jnp.where(
        lax.rem(wide, 64) < HALF, pltpu.roll(modes, 96, 1), pltpu.roll(modes, 32, 1)
    )
    low_lanes = wide < 64

    def halves(value):
        high = value.astype(jnp.bfloat16).astype(jnp.float32)
        low = value - high
        high_r, low_r = pltpu.roll(high, 64, 1), pltpu.roll(low, 64, 1)
        first = (jnp.where(low_lanes, high, low_r), high)
        second = (jnp.where(low_lanes, high_r, low), high_r)
        return first, second

    u_cos, u_sin = halves(swapped * factors[0])
    v_sin, v_cos = halves(modes * factors[1])
    wide_part = jnp.concatenate([u_cos[0], u_sin[0], v_cos[0], v_sin[0]], axis=0)
    high_part = jnp.concatenate([u_cos[1], u_sin[1], v_cos[1], v_sin[1]], axis=0)
    left = jnp.concatenate(
        [wide_part.astype(jnp.bfloat16), high_part[:, 0:64].astype(jnp.bfloat16)], axis=1
    )
    field = jnp.dot(left, tab_y[...], preferred_element_type=jnp.float32)
    for i in range(2):
        for cell in range(TILE):
            lanes = slice(cell * SLOTS, (cell + 1) * SLOTS)
            product = field[64 * i : 64 * (i + 1), lanes] * tab_x[:, lanes]
            near_uv[i, cell : cell + 1, :] = near_uv[i, cell : cell + 1, :] + jnp.sum(
                product, axis=0, keepdims=True
            )
        result = jnp.where(live, near_uv[i], 0.0)
        velocity[i] = result
        moved[i] = off[i] + section_step * result

    for sent in halo:
        sent.wait_send()

    @pl.when(is_root)
    def _():
        mate.wait_send()
        for sent in y_copies + x_copies + down_copies:
            sent.wait_send()

    @pl.when(jnp.logical_not(is_root))
    def _():
        for h in range(2):
            half_copy(h).wait_send()


def per_device(offsets, circ, counts):
    shape = jax.ShapeDtypeStruct((2, TILE, SLOTS), jnp.float32)
    vmem = pl.BlockSpec(memory_space=pltpu.VMEM)
    f32, dma = jnp.float32, pltpu.SemaphoreType.DMA
    velocity, moved = pl.pallas_call(
        kernel,
        out_shape=(shape, shape),
        in_specs=[vmem, vmem, pl.BlockSpec(memory_space=pltpu.SMEM)],
        out_specs=(vmem, vmem),
        scratch_shapes=[
            pltpu.VMEM((ROWS + 2, COLS + 2, 3, 1, SLOTS), f32),
            pltpu.VMEM((3 * TILE, SLOTS), f32),
            pltpu.VMEM((SLOTS, 3 * TILE), f32),
            pltpu.VMEM((48, SLOTS), f32),
            pltpu.VMEM((SLOTS, 48), f32),
            pltpu.VMEM((2 * TILE, 8, SLOTS), f32),
            pltpu.VMEM((2, TILE, SLOTS), f32),
            pltpu.VMEM((64, TILE * SLOTS), f32),
            pltpu.VMEM((192, TILE * SLOTS), jnp.bfloat16),
            pltpu.VMEM((128, TILE * SLOTS), jnp.bfloat16),
            pltpu.VMEM((2, HALF, 128), f32),
            pltpu.VMEM((2, 16, 128), f32),
            pltpu.VMEM((16, 16, 128), f32),
            pltpu.VMEM((8, 16, 128), f32),
            pltpu.VMEM((8, 16, 128), f32),
            pltpu.VMEM((2, 16, 128), f32),
            dma((8,)), dma((8,)), dma((2,)), dma((16,)), dma((8,)), dma((8,)), dma((8,)),
            dma((8,)), dma((8,)), dma,
            pltpu.SemaphoreType.REGULAR,
        ],
        compiler_params=pltpu.CompilerParams(
            collective_id=0, has_side_effects=True, vmem_limit_bytes=16 << 20
        ),
    )(
        offsets.reshape(2, TILE, SLOTS), circ.reshape(TILE, SLOTS), counts.reshape(TILE)
    )
    out = (2, ROWS, COLS, SLOTS)
    return velocity.reshape(out), moved.reshape(out)


def solution(mesh):
    spec = P(None, "tx", "ty", None)
    return jax.shard_map(
        per_device,
        mesh=mesh,
        in_specs=(spec, P("tx", "ty", None), P("tx", "ty")),
        out_specs=(spec, spec),
        check_vma=False,
    )
```

```python
import math

import jax
import jax.numpy as jnp
from jax import lax
from jax.experimental import pallas as pl
from jax.experimental.pallas import tpu as pltpu
from jax.sharding import PartitionSpec as P

MESH = pl.DeviceIdType.MESH
CELLS = 64
HALF = 32
ROWS, COLS = 2, 4
TILE = ROWS * COLS
SLOTS = 128
NX, NY, NZ = 4, 8, 8
TX, TY = 32, 16

two_pi = 2.0 * math.pi
screen = 1.5625
smooth = 0.0625
section_step = 0.25
alpha = screen / math.log(2.0)
sigma = math.sqrt(alpha)
near_scale = CELLS / two_pi * sigma
directions = tuple((dr, dc) for dr in (-1, 0, 1) for dc in (-1, 0, 1) if (dr, dc) != (0, 0))


def mesh_id(x, y, z, c):
    return (y * 4 + lax.rem(z, 2) * 2 + c, lax.div(z, 2) * 4 + x)


def fan(tx, ty):
    return (
        lax.rem(ty, 4),
        lax.div(tx, 4),
        lax.div(ty, 4) * 2 + lax.rem(lax.div(tx, 2), 2),
        lax.rem(tx, 2),
    )


def cos_sin(turns):
    rest = turns - jnp.round(turns)
    half = rest * math.pi
    z = half * half
    sine = half * (
        1.0
        + z
        * (
            -1.0 / 6
            + z * (1.0 / 120 + z * (-1.0 / 5040 + z * (1.0 / 362880 + z * (-1.0 / 39916800))))
        )
    )
    cosine = 1.0 + z * (
        -0.5
        + z
        * (
            1.0 / 24
            + z
            * (-1.0 / 720 + z * (1.0 / 40320 + z * (-1.0 / 3628800 + z * (1.0 / 479001600))))
        )
    )
    return 1.0 - 2.0 * sine * sine, 2.0 * sine * cosine


def split(value):
    high = value.astype(jnp.bfloat16)
    return high, (value - high.astype(jnp.float32)).astype(jnp.bfloat16)


def mode_factors():
    lane = lax.broadcasted_iota(jnp.int32, (HALF, 128), 1)
    row = lax.broadcasted_iota(jnp.int32, (HALF, 128), 0)
    wave_n = lax.rem(lane, HALF)
    k_x = two_pi * row.astype(jnp.float32)
    k_y = two_pi * wave_n.astype(jnp.float32)
    square = k_x * k_x + k_y * k_y
    keep = jnp.logical_or(row > 0, wave_n > 0)
    safe = jnp.where(keep, square, 1.0)
    damping = jnp.where(keep, jnp.exp(safe * (-1.0 / (6.25 * CELLS * CELLS))) / safe, 0.0)
    images = jnp.where(row > 0, 2.0, 1.0) * jnp.where(wave_n > 0, 2.0, 1.0)
    damping = damping * images
    for_u = damping * k_y * jnp.where(lax.rem(lane, 64) < HALF, 1.0, -1.0)
    for_v = damping * k_x * jnp.where(lane < 64, 1.0, -1.0)
    return for_u, for_v


def halo_box(dr, dc):
    src_rows = {-1: (1, 1), 0: (1, ROWS), 1: (ROWS, 1)}[dr]
    src_cols = {-1: (1, 1), 0: (1, COLS), 1: (COLS, 1)}[dc]
    dst_rows = {-1: (ROWS + 1, 1), 0: (1, ROWS), 1: (0, 1)}[dr]
    dst_cols = {-1: (COLS + 1, 1), 0: (1, COLS), 1: (0, 1)}[dc]
    return tuple(pl.ds(*a) for a in (src_rows, src_cols, dst_rows, dst_cols))


def near_targets(row, col):
    return [
        r * COLS + c
        for r in range(ROWS)
        for c in range(COLS)
        if abs(row - 1 - r) <= 1 and abs(col - 1 - c) <= 1
    ]


def add_near(sources, target, total, cells):
    used = sorted({t for cell in cells for t in cell[3]})
    target_x = {t: jnp.broadcast_to(target[t : t + 1, :], (8, SLOTS)) for t in used}
    target_y = {t: jnp.broadcast_to(target[TILE + t : TILE + t + 1, :], (8, SLOTS)) for t in used}

    def group(g, sums):
        sums = list(sums)
        block = sources[pl.ds(pl.multiple_of(g * 8, 8), 8), :]
        for at_x, at_y, at_s, targets in cells:
            source_x, source_y, strength = (
                jnp.broadcast_to(block[:, at : at + 1], (8, SLOTS)) for at in (at_x, at_y, at_s)
            )
            for t in targets:
                a = target_x[t] - source_x
                b = target_y[t] - source_y
                q = a * a + b * b
                w = strength / (jnp.exp2(q) * (q + smooth * alpha))
                sums[2 * t] = sums[2 * t] - b * w
                sums[2 * t + 1] = sums[2 * t + 1] + a * w
        return tuple(sums)

    sums = lax.fori_loop(0, SLOTS // 8, group, tuple(total[k] for k in range(2 * TILE)))
    for k in range(2 * TILE):
        total[k] = sums[k]


def kernel(
    off, circ, counts, velocity, moved,
    ext, own_rows, own_t, halo_rows, halo_t, total, near_uv, tab_x, tab_y, sided, factors,
    part, z_buf, y_buf, x_buf, final,
    halo_send, halo_recv, half_send, z_recv, y_send, y_recv, x_send, x_recv, down_send, down_recv,
    go,
):
    tx, ty = lax.axis_index("tx"), lax.axis_index("ty")
    x, y, z, c = fan(tx, ty)
    is_root = z == 0
    barrier = pltpu.get_barrier_semaphore()

    def greet(device):
        pl.semaphore_signal(barrier, inc=1, device_id=device, device_id_type=MESH)

    def copy(src, dst, send, recv, device):
        return pltpu.make_async_remote_copy(
            src_ref=src, dst_ref=dst, send_sem=send, recv_sem=recv,
            device_id=device, device_id_type=MESH,
        )

    neighbours = []
    for dr, dc in directions:
        n_tx, n_ty = lax.rem(tx + (TX + dr), TX), lax.rem(ty + (TY + dc), TY)
        neighbours.append((n_tx, n_ty))
        n_x, n_y, _, n_c = fan(n_tx, n_ty)
        greet(mesh_id(n_x, n_y, 0, n_c))

    @pl.when(jnp.logical_not(is_root))
    def _():
        greet(mesh_id(x, y, 0, c))

    @pl.when(is_root)
    def _():
        for up in range(NZ - 1, 0, -1):
            for core in range(2):
                greet(mesh_id(x, y, up, core))
        for k in range(1, NY):
            greet(mesh_id(x, lax.rem(y + k, NY), 0, c))
        for k in range(1, 2 * NX):
            greet(mesh_id(lax.rem(x + k // 2, NX), y, 0, lax.rem(c + k, 2)))

    row_of = lax.broadcasted_iota(jnp.int32, (TILE, SLOTS), 0)
    lane_of = lax.broadcasted_iota(jnp.int32, (TILE, SLOTS), 1)
    count = jnp.zeros((TILE, SLOTS), jnp.int32)
    for cell in range(TILE):
        count = jnp.where(row_of == cell, counts[cell], count)
    live = lane_of < count
    off_x, off_y = off[0], off[1]
    strength = jnp.where(live, circ[...], 0.0)
    cell_row = lax.div(row_of, COLS).astype(jnp.float32)
    cell_col = lax.rem(row_of, COLS).astype(jnp.float32)
    own_rows[2 * TILE : 3 * TILE, :] = strength

    wave = lax.broadcasted_iota(jnp.int32, (HALF, SLOTS), 0).astype(jnp.float32)
    first_col = (ty * COLS).astype(jnp.float32)
    first_row = (tx * ROWS).astype(jnp.float32)
    for cell in range(TILE):
        lanes = slice(cell * SLOTS, (cell + 1) * SLOTS)
        pos_x = (off[0, cell : cell + 1, :] + (first_col + cell % COLS)) * (1.0 / CELLS)
        pos_y = (off[1, cell : cell + 1, :] + (first_row + cell // COLS)) * (1.0 / CELLS)
        weight = own_rows[2 * TILE + cell : 2 * TILE + cell + 1, :]
        for at, table in enumerate(cos_sin(wave * pos_x)):
            rows = slice(at * HALF, (at + 1) * HALF)
            tab_x[rows, lanes] = table
            high, low = split(table * weight)
            sided[rows, lanes] = high
            sided[64 + at * HALF : 64 + (at + 1) * HALF, lanes] = low
        for at, table in enumerate(cos_sin(wave * pos_y)):
            high, low = split(table)
            tab_y[at * HALF : (at + 1) * HALF, lanes] = high
            tab_y[64 + at * HALF : 64 + (at + 1) * HALF, lanes] = high
            tab_y[128 + at * HALF : 128 + (at + 1) * HALF, lanes] = low
    sums = lax.dot_general(
        sided[...], tab_y[64:192, :], (((1,), (1,)), ((), ())),
        preferred_element_type=jnp.float32,
    )
    sums = sums[0:64] + sums[64:128]
    sums = sums + pltpu.roll(sums, 64, 1)
    wide = lax.broadcasted_iota(jnp.int32, (HALF, 128), 1)
    packed = jnp.where(wide < 64, sums[0:HALF], sums[HALF:64])
    part[0] = packed[0:16]
    part[1] = packed[16:32]

    def half_copy(h):
        return copy(
            part.at[h], z_buf.at[z * 2 + c], half_send.at[h], z_recv.at[z * 2 + c],
            mesh_id(x, y, 0, h),
        )

    @pl.when(jnp.logical_not(is_root))
    def _():
        pl.semaphore_wait(barrier, 2)
        for h in range(2):
            half_copy(h).start()

    for cell in range(TILE):
        ext[1 + cell // COLS, 1 + cell % COLS, 0] = off[0, cell : cell + 1, :]
        ext[1 + cell // COLS, 1 + cell % COLS, 1] = off[1, cell : cell + 1, :]
        ext[1 + cell // COLS, 1 + cell % COLS, 2] = own_rows[
            2 * TILE + cell : 2 * TILE + cell + 1, :
        ]
    own_rows[0:TILE, :] = (off_x + cell_col) * sigma
    own_rows[TILE : 2 * TILE, :] = (off_y + cell_row) * sigma
    own_t[...] = jnp.transpose(own_rows[...])
    total[...] = jnp.zeros_like(total)
    for_u, for_v = mode_factors()
    factors[0] = for_u
    factors[1] = for_v
    add_near(
        own_t, own_rows, total,
        [
            (k, TILE + k, 2 * TILE + k, near_targets(1 + k // COLS, 1 + k % COLS))
            for k in range(TILE)
        ],
    )

    other = 1 - c
    mate = copy(
        part.at[other], z_buf.at[c], half_send.at[0], z_recv.at[c], mesh_id(x, y, 0, other)
    )

    @pl.when(is_root)
    def _():
        pl.semaphore_wait(barrier, 64 + (NZ - 1) + (NY - 1) + (2 * NX - 1))
        mate.start()
        for up in range(1, NZ):
            pl.semaphore_signal(
                go, inc=1, device_id=mesh_id(x, y, up, c), device_id_type=MESH
            )

    @pl.when(jnp.logical_not(is_root))
    def _():
        pl.semaphore_wait(go, 1)

    halo = []
    for k, (dr, dc) in enumerate(directions):
        src_rows, src_cols, dst_rows, dst_cols = halo_box(dr, dc)
        halo.append(
            copy(
                ext.at[src_rows, src_cols], ext.at[dst_rows, dst_cols],
                halo_send.at[k], halo_recv.at[k], neighbours[k],
            )
        )
        halo[-1].start()

    y_copies = [
        copy(
            y_buf.at[y], y_buf.at[y], y_send.at[k], y_recv.at[y],
            mesh_id(x, lax.rem(y + k, NY), 0, c),
        )
        for k in range(1, NY)
    ]
    x_copies = [
        copy(
            x_buf.at[c * NX + x], x_buf.at[c * NX + x], x_send.at[k], x_recv.at[c * NX + x],
            mesh_id(lax.rem(x + k // 2, NX), y, 0, lax.rem(c + k, 2)),
        )
        for k in range(1, 2 * NX)
    ]
    down_copies = [
        copy(final, final, down_send.at[k], down_recv, mesh_id(x, y, k, c)) for k in range(1, NZ)
    ]

    @pl.when(is_root)
    def _():
        z_buf[c] = part[c]
        for up in range(1, NZ):
            for core in range(2):
                slot = up * 2 + core
                copy(part.at[0], z_buf.at[slot], half_send.at[0], z_recv.at[slot], (tx, ty)).wait_recv()
        copy(part.at[0], z_buf.at[other], half_send.at[0], z_recv.at[other], (tx, ty)).wait_recv()
        y_buf[y] = jnp.sum(z_buf[...], axis=0)
        for k in (4, 3, 5, 2, 6, 1, 7):
            y_copies[k - 1].start()
        for k in range(1, NY):
            slot = lax.rem(y + k, NY)
            copy(part.at[0], y_buf.at[slot], y_send.at[0], y_recv.at[slot], (tx, ty)).wait_recv()
        x_buf[c * NX + x] = jnp.sum(y_buf[...], axis=0)
        for k in (4, 5, 2, 3, 6, 7, 1):
            x_copies[k - 1].start()

    border = [
        (r, q) for r in range(ROWS + 2) for q in range(COLS + 2)
        if r in (0, ROWS + 1) or q in (0, COLS + 1)
    ]
    for sent in halo:
        sent.wait_recv()
    for k, (r, q) in enumerate(border):
        halo_rows[k : k + 1, :] = (ext[r, q, 0] + (q - 1.0)) * sigma
        halo_rows[16 + k : 17 + k, :] = (ext[r, q, 1] + (r - 1.0)) * sigma
        halo_rows[32 + k : 33 + k, :] = ext[r, q, 2]
    halo_t[...] = jnp.transpose(halo_rows[...])
    add_near(
        halo_t, own_rows, total,
        [(k, 16 + k, 32 + k, near_targets(r, q)) for k, (r, q) in enumerate(border)],
    )
    for t in range(TILE):
        for i in range(2):
            near_uv[i, t : t + 1, :] = jnp.sum(total[2 * t + i], axis=0, keepdims=True) * near_scale

    @pl.when(is_root)
    def _():
        for k in range(1, 2 * NX):
            slot = lax.rem(c + k, 2) * NX + lax.rem(x + k // 2, NX)
            copy(part.at[0], x_buf.at[slot], x_send.at[0], x_recv.at[slot], (tx, ty)).wait_recv()
        for h in range(2):
            final[h] = jnp.sum(x_buf[h * NX : (h + 1) * NX], axis=0)
        for k in range(1, NZ):
            down_copies[k - 1].start()

    @pl.when(jnp.logical_not(is_root))
    def _():
        down_copies[0].wait_recv()

    modes = jnp.concatenate([final[0], final[1]], axis=0)
    swapped = jnp.where(
        lax.rem(wide, 64) < HALF, pltpu.roll(modes, 96, 1), pltpu.roll(modes, 32, 1)
    )
    low_lanes = wide < 64

    def halves(value):
        high = value.astype(jnp.bfloat16).astype(jnp.float32)
        low = value - high
        high_r, low_r = pltpu.roll(high, 64, 1), pltpu.roll(low, 64, 1)
        first = (jnp.where(low_lanes, high, low_r), high)
        second = (jnp.where(low_lanes, high_r, low), high_r)
        return first, second

    u_cos, u_sin = halves(swapped * factors[0])
    v_sin, v_cos = halves(modes * factors[1])
    wide_part = jnp.concatenate([u_cos[0], u_sin[0], v_cos[0], v_sin[0]], axis=0)
    high_part = jnp.concatenate([u_cos[1], u_sin[1], v_cos[1], v_sin[1]], axis=0)
    left = jnp.concatenate(
        [wide_part.astype(jnp.bfloat16), high_part[:, 0:64].astype(jnp.bfloat16)], axis=1
    )
    field = jnp.dot(left, tab_y[...], preferred_element_type=jnp.float32)
    for i in range(2):
        for cell in range(TILE):
            lanes = slice(cell * SLOTS, (cell + 1) * SLOTS)
            product = field[64 * i : 64 * (i + 1), lanes] * tab_x[:, lanes]
            near_uv[i, cell : cell + 1, :] = near_uv[i, cell : cell + 1, :] + jnp.sum(
                product, axis=0, keepdims=True
            )
        result = jnp.where(live, near_uv[i], 0.0)
        velocity[i] = result
        moved[i] = off[i] + section_step * result

    for sent in halo:
        sent.wait_send()

    @pl.when(is_root)
    def _():
        mate.wait_send()
        for sent in y_copies + x_copies + down_copies:
            sent.wait_send()

    @pl.when(jnp.logical_not(is_root))
    def _():
        for h in range(2):
            half_copy(h).wait_send()


def per_device(offsets, circ, counts):
    shape = jax.ShapeDtypeStruct((2, TILE, SLOTS), jnp.float32)
    vmem = pl.BlockSpec(memory_space=pltpu.VMEM)
    f32, dma = jnp.float32, pltpu.SemaphoreType.DMA
    velocity, moved = pl.pallas_call(
        kernel,
        out_shape=(shape, shape),
        in_specs=[vmem, vmem, pl.BlockSpec(memory_space=pltpu.SMEM)],
        out_specs=(vmem, vmem),
        scratch_shapes=[
            pltpu.VMEM((ROWS + 2, COLS + 2, 3, 1, SLOTS), f32),
            pltpu.VMEM((3 * TILE, SLOTS), f32),
            pltpu.VMEM((SLOTS, 3 * TILE), f32),
            pltpu.VMEM((48, SLOTS), f32),
            pltpu.VMEM((SLOTS, 48), f32),
            pltpu.VMEM((2 * TILE, 8, SLOTS), f32),
            pltpu.VMEM((2, TILE, SLOTS), f32),
            pltpu.VMEM((64, TILE * SLOTS), f32),
            pltpu.VMEM((192, TILE * SLOTS), jnp.bfloat16),
            pltpu.VMEM((128, TILE * SLOTS), jnp.bfloat16),
            pltpu.VMEM((2, HALF, 128), f32),
            pltpu.VMEM((2, 16, 128), f32),
            pltpu.VMEM((16, 16, 128), f32),
            pltpu.VMEM((8, 16, 128), f32),
            pltpu.VMEM((8, 16, 128), f32),
            pltpu.VMEM((2, 16, 128), f32),
            dma((8,)), dma((8,)), dma((2,)), dma((16,)), dma((8,)), dma((8,)), dma((8,)),
            dma((8,)), dma((8,)), dma,
            pltpu.SemaphoreType.REGULAR,
        ],
        compiler_params=pltpu.CompilerParams(
            collective_id=0, has_side_effects=True, vmem_limit_bytes=16 << 20
        ),
    )(
        offsets.reshape(2, TILE, SLOTS), circ.reshape(TILE, SLOTS), counts.reshape(TILE)
    )
    out = (2, ROWS, COLS, SLOTS)
    return velocity.reshape(out), moved.reshape(out)


def solution(mesh):
    spec = P(None, "tx", "ty", None)
    return jax.shard_map(
        per_device,
        mesh=mesh,
        in_specs=(spec, P("tx", "ty", None), P("tx", "ty")),
        out_specs=(spec, spec),
        check_vma=False,
    )
```

```python
import math

import jax
import jax.numpy as jnp
from jax import lax
from jax.experimental import pallas as pl
from jax.experimental.pallas import tpu as pltpu
from jax.sharding import PartitionSpec as P

MESH = pl.DeviceIdType.MESH
CELLS = 64
HALF = 32
ROWS, COLS = 2, 4
TILE = ROWS * COLS
SLOTS = 128
NX, NY, NZ = 4, 8, 8
TX, TY = 32, 16

two_pi = 2.0 * math.pi
screen = 1.5625
smooth = 0.0625
section_step = 0.25
alpha = screen / math.log(2.0)
sigma = math.sqrt(alpha)
near_scale = CELLS / two_pi * sigma
directions = tuple((dr, dc) for dr in (-1, 0, 1) for dc in (-1, 0, 1) if (dr, dc) != (0, 0))


def mesh_id(x, y, z, c):
    return (y * 4 + lax.rem(z, 2) * 2 + c, lax.div(z, 2) * 4 + x)


def fan(tx, ty):
    return (
        lax.rem(ty, 4),
        lax.div(tx, 4),
        lax.div(ty, 4) * 2 + lax.rem(lax.div(tx, 2), 2),
        lax.rem(tx, 2),
    )


def cos_sin(turns):
    rest = turns - jnp.round(turns)
    half = rest * math.pi
    z = half * half
    sine = half * (
        1.0
        + z
        * (
            -1.0 / 6
            + z * (1.0 / 120 + z * (-1.0 / 5040 + z * (1.0 / 362880 + z * (-1.0 / 39916800))))
        )
    )
    cosine = 1.0 + z * (
        -0.5
        + z
        * (
            1.0 / 24
            + z
            * (-1.0 / 720 + z * (1.0 / 40320 + z * (-1.0 / 3628800 + z * (1.0 / 479001600))))
        )
    )
    return 1.0 - 2.0 * sine * sine, 2.0 * sine * cosine


def split(value):
    high = value.astype(jnp.bfloat16)
    return high, (value - high.astype(jnp.float32)).astype(jnp.bfloat16)


def mode_factors():
    lane = lax.broadcasted_iota(jnp.int32, (HALF, 128), 1)
    row = lax.broadcasted_iota(jnp.int32, (HALF, 128), 0)
    wave_n = lax.rem(lane, HALF)
    k_x = two_pi * row.astype(jnp.float32)
    k_y = two_pi * wave_n.astype(jnp.float32)
    square = k_x * k_x + k_y * k_y
    keep = jnp.logical_or(row > 0, wave_n > 0)
    safe = jnp.where(keep, square, 1.0)
    damping = jnp.where(keep, jnp.exp(safe * (-1.0 / (6.25 * CELLS * CELLS))) / safe, 0.0)
    images = jnp.where(row > 0, 2.0, 1.0) * jnp.where(wave_n > 0, 2.0, 1.0)
    damping = damping * images
    for_u = damping * k_y * jnp.where(lax.rem(lane, 64) < HALF, 1.0, -1.0)
    for_v = damping * k_x * jnp.where(lane < 64, 1.0, -1.0)
    return for_u, for_v


def halo_box(dr, dc):
    src_rows = {-1: (1, 1), 0: (1, ROWS), 1: (ROWS, 1)}[dr]
    src_cols = {-1: (1, 1), 0: (1, COLS), 1: (COLS, 1)}[dc]
    dst_rows = {-1: (ROWS + 1, 1), 0: (1, ROWS), 1: (0, 1)}[dr]
    dst_cols = {-1: (COLS + 1, 1), 0: (1, COLS), 1: (0, 1)}[dc]
    return tuple(pl.ds(*a) for a in (src_rows, src_cols, dst_rows, dst_cols))


def near_targets(row, col):
    return [
        r * COLS + c
        for r in range(ROWS)
        for c in range(COLS)
        if abs(row - 1 - r) <= 1 and abs(col - 1 - c) <= 1
    ]


def add_near(sources, target, total, cells):
    used = sorted({t for cell in cells for t in cell[3]})
    target_x = {t: jnp.broadcast_to(target[t : t + 1, :], (8, SLOTS)) for t in used}
    target_y = {t: jnp.broadcast_to(target[TILE + t : TILE + t + 1, :], (8, SLOTS)) for t in used}

    def group(g, sums):
        sums = list(sums)
        block = sources[pl.ds(pl.multiple_of(g * 8, 8), 8), :]
        for at_x, at_y, at_s, targets in cells:
            source_x, source_y, strength = (
                jnp.broadcast_to(block[:, at : at + 1], (8, SLOTS)) for at in (at_x, at_y, at_s)
            )
            for t in targets:
                a = target_x[t] - source_x
                b = target_y[t] - source_y
                q = a * a + b * b
                w = strength / (jnp.exp2(q) * (q + smooth * alpha))
                sums[2 * t] = sums[2 * t] - b * w
                sums[2 * t + 1] = sums[2 * t + 1] + a * w
        return tuple(sums)

    sums = lax.fori_loop(0, SLOTS // 8, group, tuple(total[k] for k in range(2 * TILE)))
    for k in range(2 * TILE):
        total[k] = sums[k]


def kernel(
    off_hbm, circ_hbm, counts_hbm, field_out,
    off, circ, counts, ext, own_rows, own_t, halo_rows, halo_t, total, near_uv, tab_x, tab_y, sided, factors,
    part, z_buf, y_buf, x_buf, final,
    halo_send, halo_recv, half_send, z_recv, y_send, y_recv, x_send, x_recv, down_send, down_recv,
    go, load,
):
    tx, ty = lax.axis_index("tx"), lax.axis_index("ty")
    x, y, z, c = fan(tx, ty)
    is_root = z == 0
    loads = [
        pltpu.make_async_copy(src, dst, load.at[k])
        for k, (src, dst) in enumerate(((counts_hbm, counts), (off_hbm, off), (circ_hbm, circ)))
    ]
    for started in loads:
        started.start()
    barrier = pltpu.get_barrier_semaphore()

    def greet(device):
        pl.semaphore_signal(barrier, inc=1, device_id=device, device_id_type=MESH)

    def copy(src, dst, send, recv, device):
        return pltpu.make_async_remote_copy(
            src_ref=src, dst_ref=dst, send_sem=send, recv_sem=recv,
            device_id=device, device_id_type=MESH,
        )

    neighbours = []
    for dr, dc in directions:
        n_tx, n_ty = lax.rem(tx + (TX + dr), TX), lax.rem(ty + (TY + dc), TY)
        neighbours.append((n_tx, n_ty))
        n_x, n_y, _, n_c = fan(n_tx, n_ty)
        greet(mesh_id(n_x, n_y, 0, n_c))

    @pl.when(jnp.logical_not(is_root))
    def _():
        greet(mesh_id(x, y, 0, c))

    @pl.when(is_root)
    def _():
        for up in range(NZ - 1, 0, -1):
            for core in range(2):
                greet(mesh_id(x, y, up, core))
        for k in range(1, NY):
            greet(mesh_id(x, lax.rem(y + k, NY), 0, c))
        for k in range(1, 2 * NX):
            greet(mesh_id(lax.rem(x + k // 2, NX), y, 0, lax.rem(c + k, 2)))

    for started in loads:
        started.wait()
    row_of = lax.broadcasted_iota(jnp.int32, (TILE, SLOTS), 0)
    lane_of = lax.broadcasted_iota(jnp.int32, (TILE, SLOTS), 1)
    count = jnp.zeros((TILE, SLOTS), jnp.int32)
    for cell in range(TILE):
        count = jnp.where(row_of == cell, counts[cell // COLS, cell % COLS], count)
    live = lane_of < count
    off_x, off_y = off[0], off[1]
    strength = jnp.where(live, circ[...], 0.0)
    cell_row = lax.div(row_of, COLS).astype(jnp.float32)
    cell_col = lax.rem(row_of, COLS).astype(jnp.float32)
    own_rows[2 * TILE : 3 * TILE, :] = strength

    wave = lax.broadcasted_iota(jnp.int32, (HALF, SLOTS), 0).astype(jnp.float32)
    first_col = (ty * COLS).astype(jnp.float32)
    first_row = (tx * ROWS).astype(jnp.float32)
    for cell in range(TILE):
        lanes = slice(cell * SLOTS, (cell + 1) * SLOTS)
        pos_x = (off[0, cell : cell + 1, :] + (first_col + cell % COLS)) * (1.0 / CELLS)
        pos_y = (off[1, cell : cell + 1, :] + (first_row + cell // COLS)) * (1.0 / CELLS)
        weight = own_rows[2 * TILE + cell : 2 * TILE + cell + 1, :]
        for at, table in enumerate(cos_sin(wave * pos_x)):
            rows = slice(at * HALF, (at + 1) * HALF)
            tab_x[rows, lanes] = table
            high, low = split(table * weight)
            sided[rows, lanes] = high
            sided[64 + at * HALF : 64 + (at + 1) * HALF, lanes] = low
        for at, table in enumerate(cos_sin(wave * pos_y)):
            high, low = split(table)
            tab_y[at * HALF : (at + 1) * HALF, lanes] = high
            tab_y[64 + at * HALF : 64 + (at + 1) * HALF, lanes] = high
            tab_y[128 + at * HALF : 128 + (at + 1) * HALF, lanes] = low
    sums = lax.dot_general(
        sided[...], tab_y[64:192, :], (((1,), (1,)), ((), ())),
        preferred_element_type=jnp.float32,
    )
    sums = sums[0:64] + sums[64:128]
    sums = sums + pltpu.roll(sums, 64, 1)
    wide = lax.broadcasted_iota(jnp.int32, (HALF, 128), 1)
    packed = jnp.where(wide < 64, sums[0:HALF], sums[HALF:64])
    part[0] = packed[0:16]
    part[1] = packed[16:32]

    def half_copy(h):
        return copy(
            part.at[h], z_buf.at[z * 2 + c], half_send.at[h], z_recv.at[z * 2 + c],
            mesh_id(x, y, 0, h),
        )

    @pl.when(jnp.logical_not(is_root))
    def _():
        pl.semaphore_wait(barrier, 2)
        for h in range(2):
            half_copy(h).start()

    for cell in range(TILE):
        ext[1 + cell // COLS, 1 + cell % COLS, 0] = off[0, cell : cell + 1, :]
        ext[1 + cell // COLS, 1 + cell % COLS, 1] = off[1, cell : cell + 1, :]
        ext[1 + cell // COLS, 1 + cell % COLS, 2] = own_rows[
            2 * TILE + cell : 2 * TILE + cell + 1, :
        ]
    own_rows[0:TILE, :] = (off_x + cell_col) * sigma
    own_rows[TILE : 2 * TILE, :] = (off_y + cell_row) * sigma
    own_t[...] = jnp.transpose(own_rows[...])
    total[...] = jnp.zeros_like(total)
    for_u, for_v = mode_factors()
    factors[0] = for_u
    factors[1] = for_v
    add_near(
        own_t, own_rows, total,
        [
            (k, TILE + k, 2 * TILE + k, near_targets(1 + k // COLS, 1 + k % COLS))
            for k in range(TILE)
        ],
    )

    other = 1 - c
    mate = copy(
        part.at[other], z_buf.at[c], half_send.at[0], z_recv.at[c], mesh_id(x, y, 0, other)
    )

    @pl.when(is_root)
    def _():
        pl.semaphore_wait(barrier, 64 + (NZ - 1) + (NY - 1) + (2 * NX - 1))
        mate.start()
        for up in range(1, NZ):
            pl.semaphore_signal(
                go, inc=1, device_id=mesh_id(x, y, up, c), device_id_type=MESH
            )

    @pl.when(jnp.logical_not(is_root))
    def _():
        pl.semaphore_wait(go, 1)

    halo = []
    for k, (dr, dc) in enumerate(directions):
        src_rows, src_cols, dst_rows, dst_cols = halo_box(dr, dc)
        halo.append(
            copy(
                ext.at[src_rows, src_cols], ext.at[dst_rows, dst_cols],
                halo_send.at[k], halo_recv.at[k], neighbours[k],
            )
        )
        halo[-1].start()

    y_copies = [
        copy(
            y_buf.at[y], y_buf.at[y], y_send.at[k], y_recv.at[y],
            mesh_id(x, lax.rem(y + k, NY), 0, c),
        )
        for k in range(1, NY)
    ]
    x_copies = [
        copy(
            x_buf.at[c * NX + x], x_buf.at[c * NX + x], x_send.at[k], x_recv.at[c * NX + x],
            mesh_id(lax.rem(x + k // 2, NX), y, 0, lax.rem(c + k, 2)),
        )
        for k in range(1, 2 * NX)
    ]
    down_copies = [
        copy(final, final, down_send.at[k], down_recv, mesh_id(x, y, k, c)) for k in range(1, NZ)
    ]

    @pl.when(is_root)
    def _():
        z_buf[c] = part[c]
        for up in range(1, NZ):
            for core in range(2):
                slot = up * 2 + core
                copy(part.at[0], z_buf.at[slot], half_send.at[0], z_recv.at[slot], (tx, ty)).wait_recv()
        copy(part.at[0], z_buf.at[other], half_send.at[0], z_recv.at[other], (tx, ty)).wait_recv()
        y_buf[y] = jnp.sum(z_buf[...], axis=0)
        for k in (4, 3, 5, 2, 6, 1, 7):
            y_copies[k - 1].start()
        for k in range(1, NY):
            slot = lax.rem(y + k, NY)
            copy(part.at[0], y_buf.at[slot], y_send.at[0], y_recv.at[slot], (tx, ty)).wait_recv()
        x_buf[c * NX + x] = jnp.sum(y_buf[...], axis=0)
        for k in (4, 5, 2, 3, 6, 7, 1):
            x_copies[k - 1].start()

    border = [
        (r, q) for r in range(ROWS + 2) for q in range(COLS + 2)
        if r in (0, ROWS + 1) or q in (0, COLS + 1)
    ]
    for sent in halo:
        sent.wait_recv()
    for k, (r, q) in enumerate(border):
        halo_rows[k : k + 1, :] = (ext[r, q, 0] + (q - 1.0)) * sigma
        halo_rows[16 + k : 17 + k, :] = (ext[r, q, 1] + (r - 1.0)) * sigma
        halo_rows[32 + k : 33 + k, :] = ext[r, q, 2]
    halo_t[...] = jnp.transpose(halo_rows[...])
    add_near(
        halo_t, own_rows, total,
        [(k, 16 + k, 32 + k, near_targets(r, q)) for k, (r, q) in enumerate(border)],
    )
    for t in range(TILE):
        for i in range(2):
            near_uv[i, t : t + 1, :] = jnp.sum(total[2 * t + i], axis=0, keepdims=True) * near_scale

    @pl.when(is_root)
    def _():
        for k in range(1, 2 * NX):
            slot = lax.rem(c + k, 2) * NX + lax.rem(x + k // 2, NX)
            copy(part.at[0], x_buf.at[slot], x_send.at[0], x_recv.at[slot], (tx, ty)).wait_recv()
        for h in range(2):
            final[h] = jnp.sum(x_buf[h * NX : (h + 1) * NX], axis=0)
        for k in range(1, NZ):
            down_copies[k - 1].start()

    @pl.when(jnp.logical_not(is_root))
    def _():
        down_copies[0].wait_recv()

    field_out[2:4] = off[...]
    field_out[4] = jnp.where(live, 1.0, 0.0)

    modes = jnp.concatenate([final[0], final[1]], axis=0)
    swapped = jnp.where(
        lax.rem(wide, 64) < HALF, pltpu.roll(modes, 96, 1), pltpu.roll(modes, 32, 1)
    )
    low_lanes = wide < 64

    def halves(value):
        high = value.astype(jnp.bfloat16).astype(jnp.float32)
        low = value - high
        high_r, low_r = pltpu.roll(high, 64, 1), pltpu.roll(low, 64, 1)
        first = (jnp.where(low_lanes, high, low_r), high)
        second = (jnp.where(low_lanes, high_r, low), high_r)
        return first, second

    u_cos, u_sin = halves(swapped * factors[0])
    v_sin, v_cos = halves(modes * factors[1])
    wide_part = jnp.concatenate([u_cos[0], u_sin[0], v_cos[0], v_sin[0]], axis=0)
    high_part = jnp.concatenate([u_cos[1], u_sin[1], v_cos[1], v_sin[1]], axis=0)
    left = jnp.concatenate(
        [wide_part.astype(jnp.bfloat16), high_part[:, 0:64].astype(jnp.bfloat16)], axis=1
    )
    field = jnp.dot(left, tab_y[...], preferred_element_type=jnp.float32)
    for i in range(2):
        for cell in range(TILE):
            lanes = slice(cell * SLOTS, (cell + 1) * SLOTS)
            product = field[64 * i : 64 * (i + 1), lanes] * tab_x[:, lanes]
            near_uv[i, cell : cell + 1, :] = near_uv[i, cell : cell + 1, :] + jnp.sum(
                product, axis=0, keepdims=True
            )
        field_out[i] = near_uv[i]

    for sent in halo:
        sent.wait_send()

    @pl.when(is_root)
    def _():
        mate.wait_send()
        for sent in y_copies + x_copies + down_copies:
            sent.wait_send()

    @pl.when(jnp.logical_not(is_root))
    def _():
        for h in range(2):
            half_copy(h).wait_send()


def per_device(offsets, circ, counts):
    shape = jax.ShapeDtypeStruct((5, TILE, SLOTS), jnp.float32)
    vmem = pl.BlockSpec(memory_space=pltpu.VMEM)
    f32, dma = jnp.float32, pltpu.SemaphoreType.DMA
    hbm = pl.BlockSpec(memory_space=pltpu.HBM)
    field = pl.pallas_call(
        kernel,
        out_shape=shape,
        in_specs=[hbm, hbm, hbm],
        out_specs=vmem,
        scratch_shapes=[
            pltpu.VMEM((2, TILE, SLOTS), f32),
            pltpu.VMEM((TILE, SLOTS), f32),
            pltpu.SMEM((ROWS, COLS), jnp.int32),
            pltpu.VMEM((ROWS + 2, COLS + 2, 3, 1, SLOTS), f32),
            pltpu.VMEM((3 * TILE, SLOTS), f32),
            pltpu.VMEM((SLOTS, 3 * TILE), f32),
            pltpu.VMEM((48, SLOTS), f32),
            pltpu.VMEM((SLOTS, 48), f32),
            pltpu.VMEM((2 * TILE, 8, SLOTS), f32),
            pltpu.VMEM((2, TILE, SLOTS), f32),
            pltpu.VMEM((64, TILE * SLOTS), f32),
            pltpu.VMEM((192, TILE * SLOTS), jnp.bfloat16),
            pltpu.VMEM((128, TILE * SLOTS), jnp.bfloat16),
            pltpu.VMEM((2, HALF, 128), f32),
            pltpu.VMEM((2, 16, 128), f32),
            pltpu.VMEM((16, 16, 128), f32),
            pltpu.VMEM((8, 16, 128), f32),
            pltpu.VMEM((8, 16, 128), f32),
            pltpu.VMEM((2, 16, 128), f32),
            dma((8,)), dma((8,)), dma((2,)), dma((16,)), dma((8,)), dma((8,)), dma((8,)),
            dma((8,)), dma((8,)), dma,
            pltpu.SemaphoreType.REGULAR, dma((3,)),
        ],
        compiler_params=pltpu.CompilerParams(
            collective_id=0, has_side_effects=True, vmem_limit_bytes=16 << 20
        ),
    )(
        *(
            pltpu.with_memory_space_constraint(value, pltpu.HBM)
            for value in (offsets.reshape(2, TILE, SLOTS), circ.reshape(TILE, SLOTS), counts)
        )
    )
    field = field.reshape((5,) + circ.shape)
    velocity = jnp.where(field[4:5] > 0.0, field[0:2], 0.0)
    return velocity, field[2:4] + section_step * velocity


def solution(mesh):
    spec = P(None, "tx", "ty", None)
    return jax.shard_map(
        per_device,
        mesh=mesh,
        in_specs=(spec, P("tx", "ty", None), P("tx", "ty")),
        out_specs=(spec, spec),
        check_vma=False,
    )
```

```python
import math

import jax
import jax.numpy as jnp
from jax import lax
from jax.experimental import pallas as pl
from jax.experimental.pallas import tpu as pltpu
from jax.sharding import PartitionSpec as P

MESH = pl.DeviceIdType.MESH
CELLS = 64
HALF = 32
ROWS, COLS = 2, 4
TILE = ROWS * COLS
SLOTS = 128
NX, NY, NZ = 4, 8, 8
TX, TY = 32, 16

two_pi = 2.0 * math.pi
screen = 1.5625
smooth = 0.0625
section_step = 0.25
alpha = screen / math.log(2.0)
sigma = math.sqrt(alpha)
near_scale = CELLS / two_pi * sigma
directions = tuple((dr, dc) for dr in (-1, 0, 1) for dc in (-1, 0, 1) if (dr, dc) != (0, 0))


def mesh_id(x, y, z, c):
    return (y * 4 + lax.rem(z, 2) * 2 + c, lax.div(z, 2) * 4 + x)


def fan(tx, ty):
    return (
        lax.rem(ty, 4),
        lax.div(tx, 4),
        lax.div(ty, 4) * 2 + lax.rem(lax.div(tx, 2), 2),
        lax.rem(tx, 2),
    )


def cos_sin(turns):
    rest = turns - jnp.round(turns)
    half = rest * math.pi
    z = half * half
    sine = half * (
        1.0
        + z
        * (
            -1.0 / 6
            + z * (1.0 / 120 + z * (-1.0 / 5040 + z * (1.0 / 362880 + z * (-1.0 / 39916800))))
        )
    )
    cosine = 1.0 + z * (
        -0.5
        + z
        * (
            1.0 / 24
            + z
            * (-1.0 / 720 + z * (1.0 / 40320 + z * (-1.0 / 3628800 + z * (1.0 / 479001600))))
        )
    )
    return 1.0 - 2.0 * sine * sine, 2.0 * sine * cosine


def split(value):
    high = value.astype(jnp.bfloat16)
    return high, (value - high.astype(jnp.float32)).astype(jnp.bfloat16)


def mode_factors():
    lane = lax.broadcasted_iota(jnp.int32, (HALF, 128), 1)
    row = lax.broadcasted_iota(jnp.int32, (HALF, 128), 0)
    wave_n = lax.rem(lane, HALF)
    k_x = two_pi * row.astype(jnp.float32)
    k_y = two_pi * wave_n.astype(jnp.float32)
    square = k_x * k_x + k_y * k_y
    keep = jnp.logical_or(row > 0, wave_n > 0)
    safe = jnp.where(keep, square, 1.0)
    damping = jnp.where(keep, jnp.exp(safe * (-1.0 / (6.25 * CELLS * CELLS))) / safe, 0.0)
    images = jnp.where(row > 0, 2.0, 1.0) * jnp.where(wave_n > 0, 2.0, 1.0)
    damping = damping * images
    for_u = damping * k_y * jnp.where(lax.rem(lane, 64) < HALF, 1.0, -1.0)
    for_v = damping * k_x * jnp.where(lane < 64, 1.0, -1.0)
    return for_u, for_v


def halo_box(dr, dc):
    src_rows = {-1: (1, 1), 0: (1, ROWS), 1: (ROWS, 1)}[dr]
    src_cols = {-1: (1, 1), 0: (1, COLS), 1: (COLS, 1)}[dc]
    dst_rows = {-1: (ROWS + 1, 1), 0: (1, ROWS), 1: (0, 1)}[dr]
    dst_cols = {-1: (COLS + 1, 1), 0: (1, COLS), 1: (0, 1)}[dc]
    return tuple(pl.ds(*a) for a in (src_rows, src_cols, dst_rows, dst_cols))


def near_targets(row, col):
    return [
        r * COLS + c
        for r in range(ROWS)
        for c in range(COLS)
        if abs(row - 1 - r) <= 1 and abs(col - 1 - c) <= 1
    ]


def add_near(sources, target, total, cells):
    used = sorted({t for cell in cells for t in cell[3]})
    target_x = {t: jnp.broadcast_to(target[t : t + 1, :], (8, SLOTS)) for t in used}
    target_y = {t: jnp.broadcast_to(target[TILE + t : TILE + t + 1, :], (8, SLOTS)) for t in used}

    at_once = 4 if sum(len(cell[3]) for cell in cells) > 20 else 8

    def groups(step, sums):
        sums = list(sums)
        for part in range(at_once):
            first = pl.multiple_of((step * at_once + part) * 8, 8)
            block = sources[pl.ds(first, 8), :]
            for at_x, at_y, at_s, targets in cells:
                source_x, source_y, strength = (
                    jnp.broadcast_to(block[:, at : at + 1], (8, SLOTS)) for at in (at_x, at_y, at_s)
                )
                for t in targets:
                    a = target_x[t] - source_x
                    b = target_y[t] - source_y
                    q = a * a + b * b
                    w = strength / (jnp.exp2(q) * (q + smooth * alpha))
                    sums[2 * t] = sums[2 * t] - b * w
                    sums[2 * t + 1] = sums[2 * t + 1] + a * w
        return tuple(sums)

    steps = SLOTS // 8 // at_once
    sums = lax.fori_loop(0, steps, groups, tuple(total[k] for k in range(2 * TILE)))
    for k in range(2 * TILE):
        total[k] = sums[k]


def kernel(
    off_hbm, circ_hbm, counts_hbm, field_out,
    off, circ, counts, ext, own_rows, own_t, halo_rows, halo_t, total, near_uv, tab_x, tab_y, sided,
    factors, part, gathered, spread, final,
    halo_send, halo_recv, part_send, part_recv, spread_send, spread_recv, down_send, down_recv, load,
    go,
):
    tx, ty = lax.axis_index("tx"), lax.axis_index("ty")
    x, y, z, c = fan(tx, ty)
    in_plane = z == 0
    is_root = jnp.logical_and(in_plane, c == 1)

    def host_row(row):
        return jnp.where(jnp.logical_or(row == 3, row == 5), 4, row)

    is_host = jnp.logical_and(jnp.logical_and(in_plane, c == 0), host_row(y) == y)
    loads = [
        pltpu.make_async_copy(src, dst, load.at[k])
        for k, (src, dst) in enumerate(((counts_hbm, counts), (off_hbm, off), (circ_hbm, circ)))
    ]
    for started in loads:
        started.start()
    barrier = pltpu.get_barrier_semaphore()

    def greet(device):
        pl.semaphore_signal(barrier, inc=1, device_id=device, device_id_type=MESH)

    def copy(src, dst, send, recv, device):
        return pltpu.make_async_remote_copy(
            src_ref=src, dst_ref=dst, send_sem=send, recv_sem=recv,
            device_id=device, device_id_type=MESH,
        )

    neighbours = [
        (lax.rem(tx + (TX + dr), TX), lax.rem(ty + (TY + dc), TY)) for dr, dc in directions
    ]
    for k, (n_tx, n_ty) in enumerate(neighbours):
        n_x, n_y, _, _ = fan(n_tx, n_ty)
        host = mesh_id(n_x, host_row(n_y), 0, 0)
        if directions[k] in ((-1, 0), (1, 0)):
            itself = jnp.logical_and(is_host, y == 4) if directions[k] == (-1, 0) else is_host

            @pl.when(jnp.logical_not(itself))
            def _(host=host):
                greet(host)
        else:
            greet(host)

    own_slot = (y * NZ + z) * 2 + c

    @pl.when(in_plane)
    def _():
        def to_roots(k, carry):
            greet(mesh_id(lax.rem(x + 1 + lax.div(k, NY), NX), lax.rem(y + k, NY), 0, 1))
            return carry

        lax.fori_loop(0, (NX - 1) * NY, to_roots, 0)

    @pl.when(is_root)
    def _():
        def to_column(k, carry):
            slot = lax.rem(own_slot + k, 2 * NY * NZ)
            greet(
                mesh_id(x, lax.div(slot, 2 * NZ), lax.rem(lax.div(slot, 2), NZ), lax.rem(slot, 2))
            )
            return carry

        lax.fori_loop(1, 2 * NY * NZ, to_column, 0)

    for started in loads:
        started.wait()
    row_of = lax.broadcasted_iota(jnp.int32, (TILE, SLOTS), 0)
    lane_of = lax.broadcasted_iota(jnp.int32, (TILE, SLOTS), 1)
    count = jnp.zeros((TILE, SLOTS), jnp.int32)
    for cell in range(TILE):
        count = jnp.where(row_of == cell, counts[cell // COLS, cell % COLS], count)
    live = lane_of < count
    off_x, off_y = off[0], off[1]
    strength = jnp.where(live, circ[...], 0.0)
    cell_row = lax.div(row_of, COLS).astype(jnp.float32)
    cell_col = lax.rem(row_of, COLS).astype(jnp.float32)
    own_rows[2 * TILE : 3 * TILE, :] = strength

    wave = lax.broadcasted_iota(jnp.int32, (HALF, SLOTS), 0).astype(jnp.float32)
    first_col = (ty * COLS).astype(jnp.float32)
    first_row = (tx * ROWS).astype(jnp.float32)
    for cell in range(TILE):
        lanes = slice(cell * SLOTS, (cell + 1) * SLOTS)
        pos_x = (off[0, cell : cell + 1, :] + (first_col + cell % COLS)) * (1.0 / CELLS)
        pos_y = (off[1, cell : cell + 1, :] + (first_row + cell // COLS)) * (1.0 / CELLS)
        weight = own_rows[2 * TILE + cell : 2 * TILE + cell + 1, :]
        for at, table in enumerate(cos_sin(wave * pos_x)):
            rows = slice(at * HALF, (at + 1) * HALF)
            tab_x[rows, lanes] = table
            high, low = split(table * weight)
            sided[rows, lanes] = high
            sided[64 + at * HALF : 64 + (at + 1) * HALF, lanes] = low
        for at, table in enumerate(cos_sin(wave * pos_y)):
            high, low = split(table)
            tab_y[at * HALF : (at + 1) * HALF, lanes] = high
            tab_y[64 + at * HALF : 64 + (at + 1) * HALF, lanes] = high
            tab_y[128 + at * HALF : 128 + (at + 1) * HALF, lanes] = low
    sums = lax.dot_general(
        sided[...], tab_y[64:192, :], (((1,), (1,)), ((), ())),
        preferred_element_type=jnp.float32,
    )
    sums = sums[0:64] + sums[64:128]
    sums = sums + pltpu.roll(sums, 64, 1)
    wide = lax.broadcasted_iota(jnp.int32, (HALF, 128), 1)
    packed = jnp.where(wide < 64, sums[0:HALF], sums[HALF:64])
    for k in range(NY):
        part[k] = packed[4 * k : 4 * k + 4]
    for cell in range(TILE):
        ext[1 + cell // COLS, 1 + cell % COLS, 0] = off[0, cell : cell + 1, :]
        ext[1 + cell // COLS, 1 + cell % COLS, 1] = off[1, cell : cell + 1, :]
        ext[1 + cell // COLS, 1 + cell % COLS, 2] = own_rows[
            2 * TILE + cell : 2 * TILE + cell + 1, :
        ]

    @pl.when(is_root)
    def _():
        pl.semaphore_wait(barrier, (NY - 1) + 2 * NY * (NX - 1))

    def part_copy(k):
        at = lax.rem(y + k, NY)
        return copy(
            part.at[at], gathered.at[own_slot], part_send.at[k], part_recv, mesh_id(x, at, 0, 1)
        )

    def send_parts():
        for k in (4, 3, 5, 2, 6, 1, 7):
            part_copy(k).start()

    @pl.when(is_root)
    def _():
        send_parts()

    @pl.when(jnp.logical_not(jnp.logical_or(is_root, is_host)))
    def _():
        pl.semaphore_wait(barrier, NY)
        send_parts()
        part_copy(0).start()

    own_rows[0:TILE, :] = (off_x + cell_col) * sigma
    own_rows[TILE : 2 * TILE, :] = (off_y + cell_row) * sigma
    own_t[...] = jnp.transpose(own_rows[...])
    total[...] = jnp.zeros_like(total)
    for_u, for_v = mode_factors()
    factors[0] = for_u
    factors[1] = for_v
    add_near(
        own_t, own_rows, total,
        [
            (k, TILE + k, 2 * TILE + k, near_targets(1 + k // COLS, 1 + k % COLS))
            for k in range(TILE)
        ],
    )

    def tell(device):
        pl.semaphore_signal(go, inc=1, device_id=device, device_id_type=MESH)

    @pl.when(is_host)
    def _():
        one_column = 2 * NZ * 8 - 1
        pl.semaphore_wait(barrier, NY + jnp.where(y == 4, 3 * one_column + 1, one_column))
        send_parts()
        part_copy(0).start()
        for k in range(1, 2 * NZ):
            tell(mesh_id(x, y, k // 2, k % 2))

        @pl.when(y == 4)
        def _():
            for k in range(2 * NZ):
                for row in (3, 5):
                    tell(mesh_id(x, row, k // 2, k % 2))

    @pl.when(jnp.logical_not(is_host))
    def _():
        pl.semaphore_wait(go, 1)

    halo = []
    for k, (dr, dc) in enumerate(directions):
        src_rows, src_cols, dst_rows, dst_cols = halo_box(dr, dc)
        halo.append(
            copy(
                ext.at[src_rows, src_cols], ext.at[dst_rows, dst_cols],
                halo_send.at[k], halo_recv.at[k], neighbours[k],
            )
        )
        halo[-1].start()

    def spread_copy(k, to_y):
        return copy(
            spread.at[y * NX + x], spread.at[y * NX + x], spread_send.at[to_y, k], spread_recv,
            mesh_id(lax.rem(x + k // 2, NX), to_y, 0, lax.rem(c + k, 2)),
        )

    @pl.when(is_root)
    def _():
        gathered[own_slot] = part[y]
        others = pl.ds(0, 2 * NY * NZ - 1)
        pltpu.make_async_copy(gathered.at[others], gathered.at[others], part_recv).wait()
        spread[y * NX + x] = jnp.sum(gathered[...], axis=0)
        for to_y in (0, 1, 2, 3, 7, 6, 5, 4):
            for k in range(1, 2 * NX):
                spread_copy(k, to_y).start()

            @pl.when(y != to_y)
            def _():
                spread_copy(0, to_y).start()

    border = [
        (r, q) for r in range(ROWS + 2) for q in range(COLS + 2)
        if r in (0, ROWS + 1) or q in (0, COLS + 1)
    ]
    for side in (0, 1, -1):
        for k, (dr, dc) in enumerate(directions):
            if dc == -side:
                halo[k].wait_recv()
        cells = [
            (r, q) for r, q in border if (q > COLS) - (q < 1) == side
        ]
        base = {0: 0, 1: 24, -1: 36}[side]
        n = len(cells)
        for k, (r, q) in enumerate(cells):
            halo_rows[base + k : base + k + 1, :] = (ext[r, q, 0] + (q - 1.0)) * sigma
            halo_rows[base + n + k : base + n + k + 1, :] = (ext[r, q, 1] + (r - 1.0)) * sigma
            halo_rows[base + 2 * n + k : base + 2 * n + k + 1, :] = ext[r, q, 2]
        rows = slice({0: 0, 1: 24, -1: 32}[side], {0: 24, 1: 40, -1: 48}[side])
        halo_t[:, rows] = jnp.transpose(halo_rows[rows, :])
        add_near(
            halo_t, own_rows, total,
            [
                (base + k, base + n + k, base + 2 * n + k, near_targets(r, q))
                for k, (r, q) in enumerate(cells)
            ],
        )
    for t in range(TILE):
        for i in range(2):
            near_uv[i, t : t + 1, :] = jnp.sum(total[2 * t + i], axis=0, keepdims=True) * near_scale

    def down_copy(k, at_y=y, core=c):
        return copy(final, final, down_send.at[k], down_recv, mesh_id(x, at_y, k % NZ, core))

    first_chip = jnp.logical_and(x == 0, y == 0)
    spared = jnp.logical_and(first_chip, c == 1)
    stands_in = jnp.logical_and(first_chip, c == 0)

    @pl.when(is_root)
    def _():
        others = pl.ds(0, NX * NY - 1)
        pltpu.make_async_copy(spread.at[others], spread.at[others], spread_recv).wait()

    @pl.when(jnp.logical_and(in_plane, c == 0))
    def _():
        pltpu.make_async_copy(spread, spread, spread_recv).wait()

    @pl.when(in_plane)
    def _():
        for k in range(NY):
            final[k] = jnp.sum(spread[k * NX : (k + 1) * NX], axis=0)
        @pl.when(stands_in)
        def _():
            for k in (1, 7, 2):
                down_copy(k + NZ, 0, 1).start()

        @pl.when(jnp.logical_not(spared))
        def _():
            for k in (1, 7, 2):
                down_copy(k).start()

        @pl.when(y != 0)
        def _():
            for k in (3, 4, 5, 6):
                down_copy(k).start()

        @pl.when(y == NY - 1)
        def _():
            for k in (3, 4, 5, 6):
                down_copy(k + NZ, 0).start()

    @pl.when(jnp.logical_not(in_plane))
    def _():
        down_copy(1).wait_recv()

    field_out[2:4] = off[...]
    field_out[4] = jnp.where(live, 1.0, 0.0)

    modes = jnp.concatenate([final[k] for k in range(NY)], axis=0)
    swapped = jnp.where(
        lax.rem(wide, 64) < HALF, pltpu.roll(modes, 96, 1), pltpu.roll(modes, 32, 1)
    )
    low_lanes = wide < 64

    def halves(value):
        high = value.astype(jnp.bfloat16).astype(jnp.float32)
        low = value - high
        high_r, low_r = pltpu.roll(high, 64, 1), pltpu.roll(low, 64, 1)
        first = (jnp.where(low_lanes, high, low_r), high)
        second = (jnp.where(low_lanes, high_r, low), high_r)
        return first, second

    u_cos, u_sin = halves(swapped * factors[0])
    v_sin, v_cos = halves(modes * factors[1])
    wide_part = jnp.concatenate([u_cos[0], u_sin[0], v_cos[0], v_sin[0]], axis=0)
    high_part = jnp.concatenate([u_cos[1], u_sin[1], v_cos[1], v_sin[1]], axis=0)
    left = jnp.concatenate(
        [wide_part.astype(jnp.bfloat16), high_part[:, 0:64].astype(jnp.bfloat16)], axis=1
    )
    field = jnp.dot(left, tab_y[...], preferred_element_type=jnp.float32)
    for i in range(2):
        for cell in range(TILE):
            lanes = slice(cell * SLOTS, (cell + 1) * SLOTS)
            product = field[64 * i : 64 * (i + 1), lanes] * tab_x[:, lanes]
            near_uv[i, cell : cell + 1, :] = near_uv[i, cell : cell + 1, :] + jnp.sum(
                product, axis=0, keepdims=True
            )
        field_out[i] = near_uv[i]

    for sent in halo:
        sent.wait_send()
    for k in range(1, NY):
        part_copy(k).wait_send()

    @pl.when(jnp.logical_not(is_root))
    def _():
        part_copy(0).wait_send()

    @pl.when(is_root)
    def _():
        for to_y in range(NY):
            for k in range(1, 2 * NX):
                spread_copy(k, to_y).wait_send()

            @pl.when(y != to_y)
            def _():
                spread_copy(0, to_y).wait_send()

    @pl.when(in_plane)
    def _():
        @pl.when(jnp.logical_not(spared))
        def _():
            for k in (1, 7, 2):
                down_copy(k).wait_send()

        @pl.when(stands_in)
        def _():
            for k in (1, 7, 2):
                down_copy(k + NZ, 0, 1).wait_send()

        @pl.when(y != 0)
        def _():
            for k in (3, 4, 5, 6):
                down_copy(k).wait_send()

        @pl.when(y == NY - 1)
        def _():
            for k in (3, 4, 5, 6):
                down_copy(k + NZ, 0).wait_send()


def per_device(offsets, circ, counts):
    shape = jax.ShapeDtypeStruct((5, TILE, SLOTS), jnp.float32)
    vmem = pl.BlockSpec(memory_space=pltpu.VMEM)
    f32, dma = jnp.float32, pltpu.SemaphoreType.DMA
    hbm = pl.BlockSpec(memory_space=pltpu.HBM)
    field = pl.pallas_call(
        kernel,
        out_shape=shape,
        in_specs=[hbm, hbm, hbm],
        out_specs=vmem,
        scratch_shapes=[
            pltpu.VMEM((2, TILE, SLOTS), f32),
            pltpu.VMEM((TILE, SLOTS), f32),
            pltpu.SMEM((ROWS, COLS), jnp.int32),
            pltpu.VMEM((ROWS + 2, COLS + 2, 3, 1, SLOTS), f32),
            pltpu.VMEM((3 * TILE, SLOTS), f32),
            pltpu.VMEM((SLOTS, 3 * TILE), f32),
            pltpu.VMEM((48, SLOTS), f32),
            pltpu.VMEM((SLOTS, 48), f32),
            pltpu.VMEM((2 * TILE, 8, SLOTS), f32),
            pltpu.VMEM((2, TILE, SLOTS), f32),
            pltpu.VMEM((64, TILE * SLOTS), f32),
            pltpu.VMEM((192, TILE * SLOTS), jnp.bfloat16),
            pltpu.VMEM((128, TILE * SLOTS), jnp.bfloat16),
            pltpu.VMEM((2, HALF, 128), f32),
            pltpu.VMEM((NY, 4, 128), f32),
            pltpu.VMEM((2 * NY * NZ, 4, 128), f32),
            pltpu.VMEM((NY * NX, 4, 128), f32),
            pltpu.VMEM((NY, 4, 128), f32),
            dma((8,)), dma((8,)), dma((NY,)), dma, dma((NY, 2 * NX)), dma, dma((2 * NZ,)), dma,
            dma((3,)), pltpu.SemaphoreType.REGULAR,
        ],
        compiler_params=pltpu.CompilerParams(
            collective_id=0, has_side_effects=True, vmem_limit_bytes=16 << 20
        ),
    )(
        *(
            pltpu.with_memory_space_constraint(value, pltpu.HBM)
            for value in (offsets.reshape(2, TILE, SLOTS), circ.reshape(TILE, SLOTS), counts)
        )
    )
    field = field.reshape((5,) + circ.shape)
    velocity = jnp.where(field[4:5] > 0.0, field[0:2], 0.0)
    return velocity, field[2:4] + section_step * velocity


def solution(mesh):
    spec = P(None, "tx", "ty", None)
    return jax.shard_map(
        per_device,
        mesh=mesh,
        in_specs=(spec, P("tx", "ty", None), P("tx", "ty")),
        out_specs=(spec, spec),
        check_vma=False,
    )
```

```python
import math

import jax
import jax.numpy as jnp
from jax import lax
from jax.experimental import pallas as pl
from jax.experimental.pallas import tpu as pltpu
from jax.sharding import PartitionSpec as P

MESH = pl.DeviceIdType.MESH
CELLS = 64
HALF = 32
ROWS, COLS = 2, 4
TILE = ROWS * COLS
SLOTS = 128
NX, NY, NZ = 4, 8, 8
TX, TY = 32, 16

two_pi = 2.0 * math.pi
screen = 1.5625
smooth = 0.0625
section_step = 0.25
alpha = screen / math.log(2.0)
sigma = math.sqrt(alpha)
near_scale = CELLS / two_pi * sigma
ROWS_FIRST = (0, 1, 2, 3, 7, 6, 5, 4)
SPREAD_ORDER = tuple(
    (x, y, c)
    for rows in ((0, 1, 2), (3, 7, 6, 5, 4))
    for columns in ((0,), (1, 2, 3))
    for y in rows
    for x in columns
    for c in (1, 0)
)
directions = tuple((dr, dc) for dr in (-1, 0, 1) for dc in (-1, 0, 1) if (dr, dc) != (0, 0))


def mesh_id(x, y, z, c):
    return (y * 4 + lax.rem(z, 2) * 2 + c, lax.div(z, 2) * 4 + x)


def fan(tx, ty):
    return (
        lax.rem(ty, 4),
        lax.div(tx, 4),
        lax.div(ty, 4) * 2 + lax.rem(lax.div(tx, 2), 2),
        lax.rem(tx, 2),
    )


def cos_sin(turns):
    rest = turns - jnp.round(turns)
    half = rest * math.pi
    z = half * half
    sine = half * (
        1.0
        + z
        * (
            -1.0 / 6
            + z * (1.0 / 120 + z * (-1.0 / 5040 + z * (1.0 / 362880 + z * (-1.0 / 39916800))))
        )
    )
    cosine = 1.0 + z * (
        -0.5
        + z
        * (
            1.0 / 24
            + z
            * (-1.0 / 720 + z * (1.0 / 40320 + z * (-1.0 / 3628800 + z * (1.0 / 479001600))))
        )
    )
    return 1.0 - 2.0 * sine * sine, 2.0 * sine * cosine


def split(value):
    high = value.astype(jnp.bfloat16)
    return high, (value - high.astype(jnp.float32)).astype(jnp.bfloat16)


def mode_factors():
    lane = lax.broadcasted_iota(jnp.int32, (HALF, 128), 1)
    row = lax.broadcasted_iota(jnp.int32, (HALF, 128), 0)
    wave_n = lax.rem(lane, HALF)
    k_x = two_pi * row.astype(jnp.float32)
    k_y = two_pi * wave_n.astype(jnp.float32)
    square = k_x * k_x + k_y * k_y
    keep = jnp.logical_or(row > 0, wave_n > 0)
    safe = jnp.where(keep, square, 1.0)
    damping = jnp.where(keep, jnp.exp(safe * (-1.0 / (6.25 * CELLS * CELLS))) / safe, 0.0)
    images = jnp.where(row > 0, 2.0, 1.0) * jnp.where(wave_n > 0, 2.0, 1.0)
    damping = damping * images
    for_u = damping * k_y * jnp.where(lax.rem(lane, 64) < HALF, 1.0, -1.0)
    for_v = damping * k_x * jnp.where(lane < 64, 1.0, -1.0)
    return for_u, for_v


def halo_box(dr, dc):
    src_rows = {-1: (1, 1), 0: (1, ROWS), 1: (ROWS, 1)}[dr]
    src_cols = {-1: (1, 1), 0: (1, COLS), 1: (COLS, 1)}[dc]
    dst_rows = {-1: (ROWS + 1, 1), 0: (1, ROWS), 1: (0, 1)}[dr]
    dst_cols = {-1: (COLS + 1, 1), 0: (1, COLS), 1: (0, 1)}[dc]
    return tuple(pl.ds(*a) for a in (src_rows, src_cols, dst_rows, dst_cols))


def near_targets(row, col):
    return [
        r * COLS + c
        for r in range(ROWS)
        for c in range(COLS)
        if abs(row - 1 - r) <= 1 and abs(col - 1 - c) <= 1
    ]


def add_near(sources, target, total, cells):
    used = sorted({t for cell in cells for t in cell[3]})
    target_x = {t: jnp.broadcast_to(target[t : t + 1, :], (8, SLOTS)) for t in used}
    target_y = {t: jnp.broadcast_to(target[TILE + t : TILE + t + 1, :], (8, SLOTS)) for t in used}

    at_once = 4 if sum(len(cell[3]) for cell in cells) > 20 else 8

    def groups(step, sums):
        sums = list(sums)
        for part in range(at_once):
            first = pl.multiple_of((step * at_once + part) * 8, 8)
            block = sources[pl.ds(first, 8), :]
            for at_x, at_y, at_s, targets in cells:
                source_x, source_y, strength = (
                    jnp.broadcast_to(block[:, at : at + 1], (8, SLOTS)) for at in (at_x, at_y, at_s)
                )
                for t in targets:
                    a = target_x[t] - source_x
                    b = target_y[t] - source_y
                    q = a * a + b * b
                    w = strength / (jnp.exp2(q) * (q + smooth * alpha))
                    sums[2 * t] = sums[2 * t] - b * w
                    sums[2 * t + 1] = sums[2 * t + 1] + a * w
        return tuple(sums)

    steps = SLOTS // 8 // at_once
    sums = lax.fori_loop(0, steps, groups, tuple(total[k] for k in range(2 * TILE)))
    for k in range(2 * TILE):
        total[k] = sums[k]


def kernel(
    off_hbm, circ_hbm, counts_hbm, field_out,
    off, circ, counts, ext, own_rows, own_t, halo_rows, halo_t, total, near_uv, tab_x, tab_y, sided,
    factors, part, gathered, spread, final,
    halo_send, halo_recv, part_send, part_recv, spread_send, spread_recv, down_send, down_recv, load,
    go,
):
    tx, ty = lax.axis_index("tx"), lax.axis_index("ty")
    x, y, z, c = fan(tx, ty)
    in_plane = z == 0
    is_root = jnp.logical_and(in_plane, c == 1)
    is_guest = jnp.logical_and(jnp.logical_and(x == 0, y == 0), z == 1)
    listens = jnp.logical_or(in_plane, is_guest)

    def host_row(row):
        return jnp.where(jnp.logical_or(row == 3, row == 5), 4, row)

    is_host = jnp.logical_and(jnp.logical_and(in_plane, c == 0), host_row(y) == y)
    loads = [
        pltpu.make_async_copy(src, dst, load.at[k])
        for k, (src, dst) in enumerate(((counts_hbm, counts), (off_hbm, off), (circ_hbm, circ)))
    ]
    for started in loads:
        started.start()
    barrier = pltpu.get_barrier_semaphore()

    def greet(device):
        pl.semaphore_signal(barrier, inc=1, device_id=device, device_id_type=MESH)

    def copy(src, dst, send, recv, device):
        return pltpu.make_async_remote_copy(
            src_ref=src, dst_ref=dst, send_sem=send, recv_sem=recv,
            device_id=device, device_id_type=MESH,
        )

    neighbours = [
        (lax.rem(tx + (TX + dr), TX), lax.rem(ty + (TY + dc), TY)) for dr, dc in directions
    ]
    for k, (n_tx, n_ty) in enumerate(neighbours):
        n_x, n_y, _, _ = fan(n_tx, n_ty)
        host = mesh_id(n_x, host_row(n_y), 0, 0)
        if directions[k] in ((-1, 0), (1, 0)):
            itself = jnp.logical_and(is_host, y == 4) if directions[k] == (-1, 0) else is_host

            @pl.when(jnp.logical_not(itself))
            def _(host=host):
                greet(host)
        else:
            greet(host)

    own_slot = (y * NZ + z) * 2 + c

    @pl.when(listens)
    def _():
        def to_roots(k, carry):
            greet(mesh_id(lax.rem(x + 1 + lax.div(k, NY), NX), lax.rem(y + k, NY), 0, 1))
            return carry

        lax.fori_loop(0, (NX - 1) * NY, to_roots, 0)

    @pl.when(is_root)
    def _():
        def to_column(k, carry):
            slot = lax.rem(own_slot + k, 2 * NY * NZ)
            greet(
                mesh_id(x, lax.div(slot, 2 * NZ), lax.rem(lax.div(slot, 2), NZ), lax.rem(slot, 2))
            )
            return carry

        lax.fori_loop(1, 2 * NY * NZ, to_column, 0)

    for started in loads:
        started.wait()
    row_of = lax.broadcasted_iota(jnp.int32, (TILE, SLOTS), 0)
    lane_of = lax.broadcasted_iota(jnp.int32, (TILE, SLOTS), 1)
    count = jnp.zeros((TILE, SLOTS), jnp.int32)
    for cell in range(TILE):
        count = jnp.where(row_of == cell, counts[cell // COLS, cell % COLS], count)
    live = lane_of < count
    off_x, off_y = off[0], off[1]
    strength = jnp.where(live, circ[...], 0.0)
    cell_row = lax.div(row_of, COLS).astype(jnp.float32)
    cell_col = lax.rem(row_of, COLS).astype(jnp.float32)
    own_rows[2 * TILE : 3 * TILE, :] = strength

    wave = lax.broadcasted_iota(jnp.int32, (HALF, SLOTS), 0).astype(jnp.float32)
    first_col = (ty * COLS).astype(jnp.float32)
    first_row = (tx * ROWS).astype(jnp.float32)
    for cell in range(TILE):
        lanes = slice(cell * SLOTS, (cell + 1) * SLOTS)
        pos_x = (off[0, cell : cell + 1, :] + (first_col + cell % COLS)) * (1.0 / CELLS)
        pos_y = (off[1, cell : cell + 1, :] + (first_row + cell // COLS)) * (1.0 / CELLS)
        weight = own_rows[2 * TILE + cell : 2 * TILE + cell + 1, :]
        for at, table in enumerate(cos_sin(wave * pos_x)):
            rows = slice(at * HALF, (at + 1) * HALF)
            tab_x[rows, lanes] = table
            high, low = split(table * weight)
            sided[rows, lanes] = high
            sided[64 + at * HALF : 64 + (at + 1) * HALF, lanes] = low
        for at, table in enumerate(cos_sin(wave * pos_y)):
            high, low = split(table)
            tab_y[at * HALF : (at + 1) * HALF, lanes] = high
            tab_y[64 + at * HALF : 64 + (at + 1) * HALF, lanes] = high
            tab_y[128 + at * HALF : 128 + (at + 1) * HALF, lanes] = low
    sums = lax.dot_general(
        sided[...], tab_y[64:192, :], (((1,), (1,)), ((), ())),
        preferred_element_type=jnp.float32,
    )
    sums = sums[0:64] + sums[64:128]
    sums = sums + pltpu.roll(sums, 64, 1)
    wide = lax.broadcasted_iota(jnp.int32, (HALF, 128), 1)
    packed = jnp.where(wide < 64, sums[0:HALF], sums[HALF:64])
    for k in range(NY):
        part[k] = packed[4 * k : 4 * k + 4]
    for cell in range(TILE):
        ext[1 + cell // COLS, 1 + cell % COLS, 0] = off[0, cell : cell + 1, :]
        ext[1 + cell // COLS, 1 + cell % COLS, 1] = off[1, cell : cell + 1, :]
        ext[1 + cell // COLS, 1 + cell % COLS, 2] = own_rows[
            2 * TILE + cell : 2 * TILE + cell + 1, :
        ]

    @pl.when(is_root)
    def _():
        pl.semaphore_wait(barrier, (NY - 1) + 2 * NY * (NX - 1) + jnp.where(x == 0, 0, 2))

    def part_copy(k):
        at = lax.rem(y + k, NY)
        return copy(
            part.at[at], gathered.at[own_slot], part_send.at[k], part_recv, mesh_id(x, at, 0, 1)
        )

    def send_parts():
        for k in (4, 3, 5, 2, 6, 1, 7):
            part_copy(k).start()

    @pl.when(is_root)
    def _():
        send_parts()

    @pl.when(jnp.logical_not(jnp.logical_or(is_root, is_host)))
    def _():
        pl.semaphore_wait(barrier, NY)
        send_parts()
        part_copy(0).start()

    own_rows[0:TILE, :] = (off_x + cell_col) * sigma
    own_rows[TILE : 2 * TILE, :] = (off_y + cell_row) * sigma
    own_t[...] = jnp.transpose(own_rows[...])
    total[...] = jnp.zeros_like(total)
    for_u, for_v = mode_factors()
    factors[0] = for_u
    factors[1] = for_v
    add_near(
        own_t, own_rows, total,
        [
            (k, TILE + k, 2 * TILE + k, near_targets(1 + k // COLS, 1 + k % COLS))
            for k in range(TILE)
        ],
    )

    def tell(device):
        pl.semaphore_signal(go, inc=1, device_id=device, device_id_type=MESH)

    @pl.when(is_host)
    def _():
        one_column = 2 * NZ * 8 - 1
        pl.semaphore_wait(barrier, NY + jnp.where(y == 4, 3 * one_column + 1, one_column))
        send_parts()
        part_copy(0).start()
        for k in range(1, 2 * NZ):
            tell(mesh_id(x, y, k // 2, k % 2))

        @pl.when(y == 4)
        def _():
            for k in range(2 * NZ):
                for row in (3, 5):
                    tell(mesh_id(x, row, k // 2, k % 2))

    @pl.when(jnp.logical_not(is_host))
    def _():
        pl.semaphore_wait(go, 1)

    halo = []
    for k, (dr, dc) in enumerate(directions):
        src_rows, src_cols, dst_rows, dst_cols = halo_box(dr, dc)
        halo.append(
            copy(
                ext.at[src_rows, src_cols], ext.at[dst_rows, dst_cols],
                halo_send.at[k], halo_recv.at[k], neighbours[k],
            )
        )
        halo[-1].start()

    def spread_copy(to_x, to_y, to_c):
        return copy(
            spread.at[y * NX + x], spread.at[y * NX + x],
            spread_send.at[to_y, 2 * to_x + to_c], spread_recv, mesh_id(to_x, to_y, 0, to_c),
        )

    def each_spread(act):
        for at, (to_x, to_y, to_c) in enumerate(SPREAD_ORDER):
            if at == 2:
                for core in range(2):
                    act(
                        copy(
                            spread.at[y * NX + x], spread.at[y * NX + x],
                            spread_send.at[NY, core], spread_recv, mesh_id(0, 0, 1, core),
                        )
                    )
            if to_c == 0:
                act(spread_copy(to_x, to_y, to_c))
            else:

                @pl.when(jnp.logical_or(x != to_x, y != to_y))
                def _(to_x=to_x, to_y=to_y, to_c=to_c):
                    act(spread_copy(to_x, to_y, to_c))

    @pl.when(is_root)
    def _():
        gathered[own_slot] = part[y]
        others = pl.ds(0, 2 * NY * NZ - 1)
        pltpu.make_async_copy(gathered.at[others], gathered.at[others], part_recv).wait()
        spread[y * NX + x] = jnp.sum(gathered[...], axis=0)
        each_spread(lambda sent: sent.start())

    border = [
        (r, q) for r in range(ROWS + 2) for q in range(COLS + 2)
        if r in (0, ROWS + 1) or q in (0, COLS + 1)
    ]
    for side in (0, 1, -1):
        for k, (dr, dc) in enumerate(directions):
            if dc == -side:
                halo[k].wait_recv()
        cells = [
            (r, q) for r, q in border if (q > COLS) - (q < 1) == side
        ]
        base = {0: 0, 1: 24, -1: 36}[side]
        n = len(cells)
        for k, (r, q) in enumerate(cells):
            halo_rows[base + k : base + k + 1, :] = (ext[r, q, 0] + (q - 1.0)) * sigma
            halo_rows[base + n + k : base + n + k + 1, :] = (ext[r, q, 1] + (r - 1.0)) * sigma
            halo_rows[base + 2 * n + k : base + 2 * n + k + 1, :] = ext[r, q, 2]
        rows = slice({0: 0, 1: 24, -1: 32}[side], {0: 24, 1: 40, -1: 48}[side])
        halo_t[:, rows] = jnp.transpose(halo_rows[rows, :])
        add_near(
            halo_t, own_rows, total,
            [
                (base + k, base + n + k, base + 2 * n + k, near_targets(r, q))
                for k, (r, q) in enumerate(cells)
            ],
        )
    for t in range(TILE):
        for i in range(2):
            near_uv[i, t : t + 1, :] = jnp.sum(total[2 * t + i], axis=0, keepdims=True) * near_scale

    def down_copy(k, at_y=y, core=c):
        return copy(final, final, down_send.at[k], down_recv, mesh_id(x, at_y, k % NZ, core))

    first_chip = jnp.logical_and(x == 0, y == 0)
    stands_in = jnp.logical_and(first_chip, c == 0)

    @pl.when(is_root)
    def _():
        others = pl.ds(0, NX * NY - 1)
        pltpu.make_async_copy(spread.at[others], spread.at[others], spread_recv).wait()

    @pl.when(jnp.logical_and(listens, jnp.logical_not(is_root)))
    def _():
        pltpu.make_async_copy(spread, spread, spread_recv).wait()

    @pl.when(listens)
    def _():
        for k in range(NY):
            final[k] = jnp.sum(spread[k * NX : (k + 1) * NX], axis=0)

    @pl.when(in_plane)
    def _():
        @pl.when(stands_in)
        def _():
            for k in (2, 7):
                down_copy(k + NZ, 0, 1).start()
                down_copy(k).start()

        @pl.when(jnp.logical_not(first_chip))
        def _():
            for k in (1, 7, 2):
                down_copy(k).start()

        @pl.when(y != 0)
        def _():
            for k in (3, 4, 5, 6):
                down_copy(k).start()

        @pl.when(y == NY - 1)
        def _():
            for k in (3, 4, 5, 6):
                down_copy(k + NZ, 0).start()

    @pl.when(jnp.logical_not(listens))
    def _():
        down_copy(1).wait_recv()

    field_out[2:4] = off[...]
    field_out[4] = jnp.where(live, 1.0, 0.0)

    modes = jnp.concatenate([final[k] for k in range(NY)], axis=0)
    swapped = jnp.where(
        lax.rem(wide, 64) < HALF, pltpu.roll(modes, 96, 1), pltpu.roll(modes, 32, 1)
    )
    low_lanes = wide < 64

    def halves(value):
        high = value.astype(jnp.bfloat16).astype(jnp.float32)
        low = value - high
        high_r, low_r = pltpu.roll(high, 64, 1), pltpu.roll(low, 64, 1)
        first = (jnp.where(low_lanes, high, low_r), high)
        second = (jnp.where(low_lanes, high_r, low), high_r)
        return first, second

    u_cos, u_sin = halves(swapped * factors[0])
    v_sin, v_cos = halves(modes * factors[1])
    wide_part = jnp.concatenate([u_cos[0], u_sin[0], v_cos[0], v_sin[0]], axis=0)
    high_part = jnp.concatenate([u_cos[1], u_sin[1], v_cos[1], v_sin[1]], axis=0)
    left = jnp.concatenate(
        [wide_part.astype(jnp.bfloat16), high_part[:, 0:64].astype(jnp.bfloat16)], axis=1
    )
    field = jnp.dot(left, tab_y[...], preferred_element_type=jnp.float32)
    for i in range(2):
        for cell in range(TILE):
            lanes = slice(cell * SLOTS, (cell + 1) * SLOTS)
            product = field[64 * i : 64 * (i + 1), lanes] * tab_x[:, lanes]
            near_uv[i, cell : cell + 1, :] = near_uv[i, cell : cell + 1, :] + jnp.sum(
                product, axis=0, keepdims=True
            )
        field_out[i] = near_uv[i]

    for sent in halo:
        sent.wait_send()
    for k in range(1, NY):
        part_copy(k).wait_send()

    @pl.when(jnp.logical_not(is_root))
    def _():
        part_copy(0).wait_send()

    @pl.when(is_root)
    def _():
        each_spread(lambda sent: sent.wait_send())

    @pl.when(in_plane)
    def _():
        @pl.when(jnp.logical_not(first_chip))
        def _():
            for k in (1, 7, 2):
                down_copy(k).wait_send()

        @pl.when(stands_in)
        def _():
            for k in (2, 7):
                down_copy(k + NZ, 0, 1).wait_send()
                down_copy(k).wait_send()

        @pl.when(y != 0)
        def _():
            for k in (3, 4, 5, 6):
                down_copy(k).wait_send()

        @pl.when(y == NY - 1)
        def _():
            for k in (3, 4, 5, 6):
                down_copy(k + NZ, 0).wait_send()


def per_device(offsets, circ, counts):
    shape = jax.ShapeDtypeStruct((5, TILE, SLOTS), jnp.float32)
    vmem = pl.BlockSpec(memory_space=pltpu.VMEM)
    f32, dma = jnp.float32, pltpu.SemaphoreType.DMA
    hbm = pl.BlockSpec(memory_space=pltpu.HBM)
    field = pl.pallas_call(
        kernel,
        out_shape=shape,
        in_specs=[hbm, hbm, hbm],
        out_specs=vmem,
        scratch_shapes=[
            pltpu.VMEM((2, TILE, SLOTS), f32),
            pltpu.VMEM((TILE, SLOTS), f32),
            pltpu.SMEM((ROWS, COLS), jnp.int32),
            pltpu.VMEM((ROWS + 2, COLS + 2, 3, 1, SLOTS), f32),
            pltpu.VMEM((3 * TILE, SLOTS), f32),
            pltpu.VMEM((SLOTS, 3 * TILE), f32),
            pltpu.VMEM((48, SLOTS), f32),
            pltpu.VMEM((SLOTS, 48), f32),
            pltpu.VMEM((2 * TILE, 8, SLOTS), f32),
            pltpu.VMEM((2, TILE, SLOTS), f32),
            pltpu.VMEM((64, TILE * SLOTS), f32),
            pltpu.VMEM((192, TILE * SLOTS), jnp.bfloat16),
            pltpu.VMEM((128, TILE * SLOTS), jnp.bfloat16),
            pltpu.VMEM((2, HALF, 128), f32),
            pltpu.VMEM((NY, 4, 128), f32),
            pltpu.VMEM((2 * NY * NZ, 4, 128), f32),
            pltpu.VMEM((NY * NX, 4, 128), f32),
            pltpu.VMEM((NY, 4, 128), f32),
            dma((8,)), dma((8,)), dma((NY,)), dma, dma((NY + 1, 2 * NX)), dma, dma((2 * NZ,)), dma,
            dma((3,)), pltpu.SemaphoreType.REGULAR,
        ],
        compiler_params=pltpu.CompilerParams(
            collective_id=0, has_side_effects=True, vmem_limit_bytes=16 << 20
        ),
    )(
        *(
            pltpu.with_memory_space_constraint(value, pltpu.HBM)
            for value in (offsets.reshape(2, TILE, SLOTS), circ.reshape(TILE, SLOTS), counts)
        )
    )
    field = field.reshape((5,) + circ.shape)
    velocity = jnp.where(field[4:5] > 0.0, field[0:2], 0.0)
    return velocity, field[2:4] + section_step * velocity


def solution(mesh):
    spec = P(None, "tx", "ty", None)
    return jax.shard_map(
        per_device,
        mesh=mesh,
        in_specs=(spec, P("tx", "ty", None), P("tx", "ty")),
        out_specs=(spec, spec),
        check_vma=False,
    )
```

```python
import math

import jax
import jax.numpy as jnp
from jax import lax
from jax.experimental import pallas as pl
from jax.experimental.pallas import tpu as pltpu
from jax.sharding import PartitionSpec as P

MESH = pl.DeviceIdType.MESH
CELLS = 64
HALF = 32
ROWS, COLS = 2, 4
TILE = ROWS * COLS
SLOTS = 128
NX, NY, NZ = 4, 8, 8
TX, TY = 32, 16

two_pi = 2.0 * math.pi
screen = 1.5625
smooth = 0.0625
section_step = 0.25
alpha = screen / math.log(2.0)
sigma = math.sqrt(alpha)
near_scale = CELLS / two_pi * sigma
ROWS_FIRST = (0, 1, 2, 3, 7, 6, 5, 4)
SPREAD_ORDER = tuple(
    (x, y, c)
    for rows in ((0, 1, 2), (3, 7, 6, 5, 4))
    for columns in ((0,), (1, 2, 3))
    for y in rows
    for x in columns
    for c in (1, 0)
)
directions = tuple((dr, dc) for dr in (-1, 0, 1) for dc in (-1, 0, 1) if (dr, dc) != (0, 0))


def mesh_id(x, y, z, c):
    return (y * 4 + lax.rem(z, 2) * 2 + c, lax.div(z, 2) * 4 + x)


def fan(tx, ty):
    return (
        lax.rem(ty, 4),
        lax.div(tx, 4),
        lax.div(ty, 4) * 2 + lax.rem(lax.div(tx, 2), 2),
        lax.rem(tx, 2),
    )


def cos_sin(turns):
    rest = turns - jnp.round(turns)
    half = rest * math.pi
    z = half * half
    sine = half * (
        1.0
        + z
        * (
            -1.0 / 6
            + z * (1.0 / 120 + z * (-1.0 / 5040 + z * (1.0 / 362880 + z * (-1.0 / 39916800))))
        )
    )
    cosine = 1.0 + z * (
        -0.5
        + z
        * (
            1.0 / 24
            + z
            * (-1.0 / 720 + z * (1.0 / 40320 + z * (-1.0 / 3628800 + z * (1.0 / 479001600))))
        )
    )
    return 1.0 - 2.0 * sine * sine, 2.0 * sine * cosine


def wave_tables(position):
    few = lax.broadcasted_iota(jnp.int32, (8, SLOTS), 0).astype(jnp.float32)
    cos_few, sin_few = cos_sin(few * position)
    cos_step, sin_step = cos_sin(few * (8.0 * position))
    cosines, sines = [cos_few], [sin_few]
    for k in range(1, HALF // 8):
        cos_k, sin_k = cos_step[k : k + 1], sin_step[k : k + 1]
        cosines.append(cos_k * cos_few - sin_k * sin_few)
        sines.append(sin_k * cos_few + cos_k * sin_few)
    return jnp.concatenate(cosines, axis=0), jnp.concatenate(sines, axis=0)


def split(value):
    high = value.astype(jnp.bfloat16)
    return high, (value - high.astype(jnp.float32)).astype(jnp.bfloat16)


def mode_factors():
    lane = lax.broadcasted_iota(jnp.int32, (HALF, 128), 1)
    row = lax.broadcasted_iota(jnp.int32, (HALF, 128), 0)
    wave_n = lax.rem(lane, HALF)
    k_x = two_pi * row.astype(jnp.float32)
    k_y = two_pi * wave_n.astype(jnp.float32)
    square = k_x * k_x + k_y * k_y
    keep = jnp.logical_or(row > 0, wave_n > 0)
    safe = jnp.where(keep, square, 1.0)
    damping = jnp.where(keep, jnp.exp(safe * (-1.0 / (6.25 * CELLS * CELLS))) / safe, 0.0)
    images = jnp.where(row > 0, 2.0, 1.0) * jnp.where(wave_n > 0, 2.0, 1.0)
    damping = damping * images
    for_u = damping * k_y * jnp.where(lax.rem(lane, 64) < HALF, 1.0, -1.0)
    for_v = damping * k_x * jnp.where(lane < 64, 1.0, -1.0)
    return for_u, for_v


def halo_box(dr, dc):
    src_rows = {-1: (1, 1), 0: (1, ROWS), 1: (ROWS, 1)}[dr]
    src_cols = {-1: (1, 1), 0: (1, COLS), 1: (COLS, 1)}[dc]
    dst_rows = {-1: (ROWS + 1, 1), 0: (1, ROWS), 1: (0, 1)}[dr]
    dst_cols = {-1: (COLS + 1, 1), 0: (1, COLS), 1: (0, 1)}[dc]
    return tuple(pl.ds(*a) for a in (src_rows, src_cols, dst_rows, dst_cols))


def near_targets(row, col):
    return [
        r * COLS + c
        for r in range(ROWS)
        for c in range(COLS)
        if abs(row - 1 - r) <= 1 and abs(col - 1 - c) <= 1
    ]


def add_near(sources, target, total, cells):
    used = sorted({t for cell in cells for t in cell[3]})
    target_x = {t: jnp.broadcast_to(target[t : t + 1, :], (8, SLOTS)) for t in used}
    target_y = {t: jnp.broadcast_to(target[TILE + t : TILE + t + 1, :], (8, SLOTS)) for t in used}

    at_once = 4 if sum(len(cell[3]) for cell in cells) > 20 else 8

    def groups(step, sums):
        sums = list(sums)
        for part in range(at_once):
            first = pl.multiple_of((step * at_once + part) * 8, 8)
            block = sources[pl.ds(first, 8), :]
            for at_x, at_y, at_s, targets in cells:
                source_x, source_y, strength = (
                    jnp.broadcast_to(block[:, at : at + 1], (8, SLOTS)) for at in (at_x, at_y, at_s)
                )
                for t in targets:
                    a = target_x[t] - source_x
                    b = target_y[t] - source_y
                    q = a * a + b * b
                    w = strength / (jnp.exp2(q) * (q + smooth * alpha))
                    sums[2 * t] = sums[2 * t] - b * w
                    sums[2 * t + 1] = sums[2 * t + 1] + a * w
        return tuple(sums)

    steps = SLOTS // 8 // at_once
    sums = lax.fori_loop(0, steps, groups, tuple(total[k] for k in range(2 * TILE)))
    for k in range(2 * TILE):
        total[k] = sums[k]


def kernel(
    off_hbm, circ_hbm, counts_hbm, field_out,
    off, circ, counts, ext, own_rows, own_t, halo_rows, halo_t, total, near_uv, tab_x, tab_y, sided,
    factors, part, gathered, spread, final,
    halo_send, halo_recv, part_send, part_recv, spread_send, spread_recv, down_send, down_recv, load,
    go,
):
    tx, ty = lax.axis_index("tx"), lax.axis_index("ty")
    x, y, z, c = fan(tx, ty)
    in_plane = z == 0
    is_root = jnp.logical_and(in_plane, c == 1)
    is_guest = jnp.logical_and(jnp.logical_and(x == 0, y == 0), z == 1)
    listens = jnp.logical_or(in_plane, is_guest)

    def host_row(row):
        return jnp.where(jnp.logical_or(row == 3, row == 5), 4, row)

    is_host = jnp.logical_and(jnp.logical_and(in_plane, c == 0), host_row(y) == y)
    loads = [
        pltpu.make_async_copy(src, dst, load.at[k])
        for k, (src, dst) in enumerate(((counts_hbm, counts), (off_hbm, off), (circ_hbm, circ)))
    ]
    for started in loads:
        started.start()
    barrier = pltpu.get_barrier_semaphore()

    def greet(device):
        pl.semaphore_signal(barrier, inc=1, device_id=device, device_id_type=MESH)

    def copy(src, dst, send, recv, device):
        return pltpu.make_async_remote_copy(
            src_ref=src, dst_ref=dst, send_sem=send, recv_sem=recv,
            device_id=device, device_id_type=MESH,
        )

    neighbours = [
        (lax.rem(tx + (TX + dr), TX), lax.rem(ty + (TY + dc), TY)) for dr, dc in directions
    ]
    for k, (n_tx, n_ty) in enumerate(neighbours):
        n_x, n_y, _, _ = fan(n_tx, n_ty)
        host = mesh_id(n_x, host_row(n_y), 0, 0)
        if directions[k] in ((-1, 0), (1, 0)):
            itself = jnp.logical_and(is_host, y == 4) if directions[k] == (-1, 0) else is_host

            @pl.when(jnp.logical_not(itself))
            def _(host=host):
                greet(host)
        else:
            greet(host)

    own_slot = (y * NZ + z) * 2 + c

    @pl.when(listens)
    def _():
        def to_roots(k, carry):
            greet(mesh_id(lax.rem(x + 1 + lax.div(k, NY), NX), lax.rem(y + k, NY), 0, 1))
            return carry

        lax.fori_loop(0, (NX - 1) * NY, to_roots, 0)

    @pl.when(is_root)
    def _():
        def to_column(k, carry):
            slot = lax.rem(own_slot + k, 2 * NY * NZ)
            greet(
                mesh_id(x, lax.div(slot, 2 * NZ), lax.rem(lax.div(slot, 2), NZ), lax.rem(slot, 2))
            )
            return carry

        lax.fori_loop(1, 2 * NY * NZ, to_column, 0)

    for started in loads:
        started.wait()
    row_of = lax.broadcasted_iota(jnp.int32, (TILE, SLOTS), 0)
    lane_of = lax.broadcasted_iota(jnp.int32, (TILE, SLOTS), 1)
    count = jnp.zeros((TILE, SLOTS), jnp.int32)
    for cell in range(TILE):
        count = jnp.where(row_of == cell, counts[cell // COLS, cell % COLS], count)
    live = lane_of < count
    off_x, off_y = off[0], off[1]
    strength = jnp.where(live, circ[...], 0.0)
    cell_row = lax.div(row_of, COLS).astype(jnp.float32)
    cell_col = lax.rem(row_of, COLS).astype(jnp.float32)
    own_rows[2 * TILE : 3 * TILE, :] = strength

    first_col = (ty * COLS).astype(jnp.float32)
    first_row = (tx * ROWS).astype(jnp.float32)
    for cell in range(TILE):
        lanes = slice(cell * SLOTS, (cell + 1) * SLOTS)
        pos_x = (off[0, cell : cell + 1, :] + (first_col + cell % COLS)) * (1.0 / CELLS)
        pos_y = (off[1, cell : cell + 1, :] + (first_row + cell // COLS)) * (1.0 / CELLS)
        weight = own_rows[2 * TILE + cell : 2 * TILE + cell + 1, :]
        for at, table in enumerate(wave_tables(pos_x)):
            rows = slice(at * HALF, (at + 1) * HALF)
            tab_x[rows, lanes] = table
            high, low = split(table * weight)
            sided[rows, lanes] = high
            sided[64 + at * HALF : 64 + (at + 1) * HALF, lanes] = low
        for at, table in enumerate(wave_tables(pos_y)):
            high, low = split(table)
            tab_y[at * HALF : (at + 1) * HALF, lanes] = high
            tab_y[64 + at * HALF : 64 + (at + 1) * HALF, lanes] = high
            tab_y[128 + at * HALF : 128 + (at + 1) * HALF, lanes] = low
    sums = lax.dot_general(
        sided[...], tab_y[64:192, :], (((1,), (1,)), ((), ())),
        preferred_element_type=jnp.float32,
    )
    sums = sums[0:64] + sums[64:128]
    sums = sums + pltpu.roll(sums, 64, 1)
    wide = lax.broadcasted_iota(jnp.int32, (HALF, 128), 1)
    packed = jnp.where(wide < 64, sums[0:HALF], sums[HALF:64])
    for k in range(NY):
        part[k] = packed[4 * k : 4 * k + 4]
    for cell in range(TILE):
        ext[1 + cell // COLS, 1 + cell % COLS, 0] = off[0, cell : cell + 1, :]
        ext[1 + cell // COLS, 1 + cell % COLS, 1] = off[1, cell : cell + 1, :]
        ext[1 + cell // COLS, 1 + cell % COLS, 2] = own_rows[
            2 * TILE + cell : 2 * TILE + cell + 1, :
        ]

    @pl.when(is_root)
    def _():
        pl.semaphore_wait(barrier, (NY - 1) + 2 * NY * (NX - 1) + jnp.where(x == 0, 0, 2))

    def part_copy(k):
        at = lax.rem(y + k, NY)
        return copy(
            part.at[at], gathered.at[own_slot], part_send.at[k], part_recv, mesh_id(x, at, 0, 1)
        )

    def send_parts():
        for k in (4, 3, 5, 2, 6, 1, 7):
            part_copy(k).start()

    @pl.when(is_root)
    def _():
        send_parts()

    @pl.when(jnp.logical_not(jnp.logical_or(is_root, is_host)))
    def _():
        pl.semaphore_wait(barrier, NY)
        send_parts()
        part_copy(0).start()

    own_rows[0:TILE, :] = (off_x + cell_col) * sigma
    own_rows[TILE : 2 * TILE, :] = (off_y + cell_row) * sigma
    own_t[...] = jnp.transpose(own_rows[...])
    total[...] = jnp.zeros_like(total)
    for_u, for_v = mode_factors()
    factors[0] = for_u
    factors[1] = for_v
    add_near(
        own_t, own_rows, total,
        [
            (k, TILE + k, 2 * TILE + k, near_targets(1 + k // COLS, 1 + k % COLS))
            for k in range(TILE)
        ],
    )

    def tell(device):
        pl.semaphore_signal(go, inc=1, device_id=device, device_id_type=MESH)

    @pl.when(is_host)
    def _():
        one_column = 2 * NZ * 8 - 1
        pl.semaphore_wait(barrier, NY + jnp.where(y == 4, 3 * one_column + 1, one_column))
        send_parts()
        part_copy(0).start()
        for k in range(1, 2 * NZ):
            tell(mesh_id(x, y, k // 2, k % 2))

        @pl.when(y == 4)
        def _():
            for k in range(2 * NZ):
                for row in (3, 5):
                    tell(mesh_id(x, row, k // 2, k % 2))

    @pl.when(jnp.logical_not(is_host))
    def _():
        pl.semaphore_wait(go, 1)

    halo = []
    for k, (dr, dc) in enumerate(directions):
        src_rows, src_cols, dst_rows, dst_cols = halo_box(dr, dc)
        halo.append(
            copy(
                ext.at[src_rows, src_cols], ext.at[dst_rows, dst_cols],
                halo_send.at[k], halo_recv.at[k], neighbours[k],
            )
        )
        halo[-1].start()

    def spread_copy(to_x, to_y, to_c):
        return copy(
            spread.at[y * NX + x], spread.at[y * NX + x],
            spread_send.at[to_y, 2 * to_x + to_c], spread_recv, mesh_id(to_x, to_y, 0, to_c),
        )

    def each_spread(act):
        for at, (to_x, to_y, to_c) in enumerate(SPREAD_ORDER):
            if at == 2:
                for core in range(2):
                    act(
                        copy(
                            spread.at[y * NX + x], spread.at[y * NX + x],
                            spread_send.at[NY, core], spread_recv, mesh_id(0, 0, 1, core),
                        )
                    )
            if to_c == 0:
                act(spread_copy(to_x, to_y, to_c))
            else:

                @pl.when(jnp.logical_or(x != to_x, y != to_y))
                def _(to_x=to_x, to_y=to_y, to_c=to_c):
                    act(spread_copy(to_x, to_y, to_c))

    @pl.when(is_root)
    def _():
        gathered[own_slot] = part[y]
        others = pl.ds(0, 2 * NY * NZ - 1)
        pltpu.make_async_copy(gathered.at[others], gathered.at[others], part_recv).wait()
        some = [gathered[k : k + 16] for k in range(0, 2 * NY * NZ, 16)]
        while len(some) > 1:
            some = [some[k] + some[k + 1] for k in range(0, len(some), 2)]
        whole = some[0]
        while whole.shape[0] > 1:
            half = whole.shape[0] // 2
            whole = whole[:half] + whole[half:]
        spread[y * NX + x] = whole[0]
        each_spread(lambda sent: sent.start())

    border = [
        (r, q) for r in range(ROWS + 2) for q in range(COLS + 2)
        if r in (0, ROWS + 1) or q in (0, COLS + 1)
    ]
    for side in (0, 1, -1):
        for k, (dr, dc) in enumerate(directions):
            if dc == -side:
                halo[k].wait_recv()
        cells = [
            (r, q) for r, q in border if (q > COLS) - (q < 1) == side
        ]
        base = {0: 0, 1: 24, -1: 36}[side]
        n = len(cells)
        for k, (r, q) in enumerate(cells):
            halo_rows[base + k : base + k + 1, :] = (ext[r, q, 0] + (q - 1.0)) * sigma
            halo_rows[base + n + k : base + n + k + 1, :] = (ext[r, q, 1] + (r - 1.0)) * sigma
            halo_rows[base + 2 * n + k : base + 2 * n + k + 1, :] = ext[r, q, 2]
        rows = slice({0: 0, 1: 24, -1: 32}[side], {0: 24, 1: 40, -1: 48}[side])
        halo_t[:, rows] = jnp.transpose(halo_rows[rows, :])
        add_near(
            halo_t, own_rows, total,
            [
                (base + k, base + n + k, base + 2 * n + k, near_targets(r, q))
                for k, (r, q) in enumerate(cells)
            ],
        )
    for t in range(TILE):
        for i in range(2):
            near_uv[i, t : t + 1, :] = jnp.sum(total[2 * t + i], axis=0, keepdims=True) * near_scale

    def down_copy(k, at_y=y, core=c):
        return copy(final, final, down_send.at[k], down_recv, mesh_id(x, at_y, k % NZ, core))

    first_chip = jnp.logical_and(x == 0, y == 0)
    stands_in = jnp.logical_and(first_chip, c == 0)

    @pl.when(is_root)
    def _():
        others = pl.ds(0, NX * NY - 1)
        pltpu.make_async_copy(spread.at[others], spread.at[others], spread_recv).wait()

    @pl.when(jnp.logical_and(listens, jnp.logical_not(is_root)))
    def _():
        pltpu.make_async_copy(spread, spread, spread_recv).wait()

    @pl.when(listens)
    def _():
        for k in range(NY):
            final[k] = jnp.sum(spread[k * NX : (k + 1) * NX], axis=0)

    @pl.when(in_plane)
    def _():
        @pl.when(stands_in)
        def _():
            for k in (2, 7):
                down_copy(k + NZ, 0, 1).start()
                down_copy(k).start()

        @pl.when(jnp.logical_not(first_chip))
        def _():
            for k in (1, 7, 2):
                down_copy(k).start()

        @pl.when(y != 0)
        def _():
            for k in (3, 4, 5, 6):
                down_copy(k).start()

        @pl.when(y == NY - 1)
        def _():
            for k in (3, 4, 5, 6):
                down_copy(k + NZ, 0).start()

    @pl.when(jnp.logical_not(listens))
    def _():
        down_copy(1).wait_recv()

    field_out[2:4] = off[...]
    field_out[4] = jnp.where(live, 1.0, 0.0)

    modes = jnp.concatenate([final[k] for k in range(NY)], axis=0)
    swapped = jnp.where(
        lax.rem(wide, 64) < HALF, pltpu.roll(modes, 96, 1), pltpu.roll(modes, 32, 1)
    )
    low_lanes = wide < 64

    def halves(value):
        high = value.astype(jnp.bfloat16).astype(jnp.float32)
        low = value - high
        high_r, low_r = pltpu.roll(high, 64, 1), pltpu.roll(low, 64, 1)
        first = (jnp.where(low_lanes, high, low_r), high)
        second = (jnp.where(low_lanes, high_r, low), high_r)
        return first, second

    u_cos, u_sin = halves(swapped * factors[0])
    v_sin, v_cos = halves(modes * factors[1])
    wide_part = jnp.concatenate([u_cos[0], u_sin[0], v_cos[0], v_sin[0]], axis=0)
    high_part = jnp.concatenate([u_cos[1], u_sin[1], v_cos[1], v_sin[1]], axis=0)
    left = jnp.concatenate(
        [wide_part.astype(jnp.bfloat16), high_part[:, 0:64].astype(jnp.bfloat16)], axis=1
    )
    field = jnp.dot(left, tab_y[...], preferred_element_type=jnp.float32)
    for i in range(2):
        for cell in range(TILE):
            lanes = slice(cell * SLOTS, (cell + 1) * SLOTS)
            product = field[64 * i : 64 * (i + 1), lanes] * tab_x[:, lanes]
            near_uv[i, cell : cell + 1, :] = near_uv[i, cell : cell + 1, :] + jnp.sum(
                product, axis=0, keepdims=True
            )
        field_out[i] = near_uv[i]

    for sent in halo:
        sent.wait_send()
    for k in range(1, NY):
        part_copy(k).wait_send()

    @pl.when(jnp.logical_not(is_root))
    def _():
        part_copy(0).wait_send()

    @pl.when(is_root)
    def _():
        each_spread(lambda sent: sent.wait_send())

    @pl.when(in_plane)
    def _():
        @pl.when(jnp.logical_not(first_chip))
        def _():
            for k in (1, 7, 2):
                down_copy(k).wait_send()

        @pl.when(stands_in)
        def _():
            for k in (2, 7):
                down_copy(k + NZ, 0, 1).wait_send()
                down_copy(k).wait_send()

        @pl.when(y != 0)
        def _():
            for k in (3, 4, 5, 6):
                down_copy(k).wait_send()

        @pl.when(y == NY - 1)
        def _():
            for k in (3, 4, 5, 6):
                down_copy(k + NZ, 0).wait_send()


def per_device(offsets, circ, counts):
    shape = jax.ShapeDtypeStruct((5, TILE, SLOTS), jnp.float32)
    vmem = pl.BlockSpec(memory_space=pltpu.VMEM)
    f32, dma = jnp.float32, pltpu.SemaphoreType.DMA
    hbm = pl.BlockSpec(memory_space=pltpu.HBM)
    field = pl.pallas_call(
        kernel,
        out_shape=shape,
        in_specs=[hbm, hbm, hbm],
        out_specs=vmem,
        scratch_shapes=[
            pltpu.VMEM((2, TILE, SLOTS), f32),
            pltpu.VMEM((TILE, SLOTS), f32),
            pltpu.SMEM((ROWS, COLS), jnp.int32),
            pltpu.VMEM((ROWS + 2, COLS + 2, 3, 1, SLOTS), f32),
            pltpu.VMEM((3 * TILE, SLOTS), f32),
            pltpu.VMEM((SLOTS, 3 * TILE), f32),
            pltpu.VMEM((48, SLOTS), f32),
            pltpu.VMEM((SLOTS, 48), f32),
            pltpu.VMEM((2 * TILE, 8, SLOTS), f32),
            pltpu.VMEM((2, TILE, SLOTS), f32),
            pltpu.VMEM((64, TILE * SLOTS), f32),
            pltpu.VMEM((192, TILE * SLOTS), jnp.bfloat16),
            pltpu.VMEM((128, TILE * SLOTS), jnp.bfloat16),
            pltpu.VMEM((2, HALF, 128), f32),
            pltpu.VMEM((NY, 4, 128), f32),
            pltpu.VMEM((2 * NY * NZ, 4, 128), f32),
            pltpu.VMEM((NY * NX, 4, 128), f32),
            pltpu.VMEM((NY, 4, 128), f32),
            dma((8,)), dma((8,)), dma((NY,)), dma, dma((NY + 1, 2 * NX)), dma, dma((2 * NZ,)), dma,
            dma((3,)), pltpu.SemaphoreType.REGULAR,
        ],
        compiler_params=pltpu.CompilerParams(
            collective_id=0, has_side_effects=True, vmem_limit_bytes=16 << 20
        ),
    )(
        *(
            pltpu.with_memory_space_constraint(value, pltpu.HBM)
            for value in (offsets.reshape(2, TILE, SLOTS), circ.reshape(TILE, SLOTS), counts)
        )
    )
    field = field.reshape((5,) + circ.shape)
    velocity = jnp.where(field[4:5] > 0.0, field[0:2], 0.0)
    return velocity, field[2:4] + section_step * velocity


def solution(mesh):
    spec = P(None, "tx", "ty", None)
    return jax.shard_map(
        per_device,
        mesh=mesh,
        in_specs=(spec, P("tx", "ty", None), P("tx", "ty")),
        out_specs=(spec, spec),
        check_vma=False,
    )
```

```python
import math

import jax
import jax.numpy as jnp
from jax import lax
from jax.experimental import pallas as pl
from jax.experimental.pallas import tpu as pltpu
from jax.sharding import PartitionSpec as P

MESH = pl.DeviceIdType.MESH
CELLS = 64
HALF = 32
ROWS, COLS = 2, 4
TILE = ROWS * COLS
SLOTS = 128
NX, NY, NZ = 4, 8, 8
TX, TY = 32, 16

two_pi = 2.0 * math.pi
screen = 1.5625
smooth = 0.0625
section_step = 0.25
alpha = screen / math.log(2.0)
sigma = math.sqrt(alpha)
near_scale = CELLS / two_pi * sigma
ROWS_FIRST = (0, 1, 2, 3, 7, 6, 5, 4)
SPREAD_ORDER = tuple(
    (x, y, c)
    for rows in ((0, 1, 2), (3, 7, 6, 5, 4))
    for columns in ((0,), (1, 2, 3))
    for y in rows
    for x in columns
    for c in (1, 0)
)
directions = tuple((dr, dc) for dr in (-1, 0, 1) for dc in (-1, 0, 1) if (dr, dc) != (0, 0))


def mesh_id(x, y, z, c):
    return (y * 4 + lax.rem(z, 2) * 2 + c, lax.div(z, 2) * 4 + x)


def fan(tx, ty):
    return (
        lax.rem(ty, 4),
        lax.div(tx, 4),
        lax.div(ty, 4) * 2 + lax.rem(lax.div(tx, 2), 2),
        lax.rem(tx, 2),
    )


def cos_sin(turns):
    rest = turns - jnp.round(turns)
    half = rest * math.pi
    z = half * half
    sine = half * (
        1.0
        + z
        * (
            -1.0 / 6
            + z * (1.0 / 120 + z * (-1.0 / 5040 + z * (1.0 / 362880 + z * (-1.0 / 39916800))))
        )
    )
    cosine = 1.0 + z * (
        -0.5
        + z
        * (
            1.0 / 24
            + z
            * (-1.0 / 720 + z * (1.0 / 40320 + z * (-1.0 / 3628800 + z * (1.0 / 479001600))))
        )
    )
    return 1.0 - 2.0 * sine * sine, 2.0 * sine * cosine


def wave_tables(position):
    few = lax.broadcasted_iota(jnp.int32, (8, SLOTS), 0).astype(jnp.float32)
    cos_few, sin_few = cos_sin(few * position)
    cos_step, sin_step = cos_sin(few * (8.0 * position))
    cosines, sines = [cos_few], [sin_few]
    for k in range(1, HALF // 8):
        cos_k, sin_k = cos_step[k : k + 1], sin_step[k : k + 1]
        cosines.append(cos_k * cos_few - sin_k * sin_few)
        sines.append(sin_k * cos_few + cos_k * sin_few)
    return jnp.concatenate(cosines, axis=0), jnp.concatenate(sines, axis=0)


def split(value):
    high = value.astype(jnp.bfloat16)
    return high, (value - high.astype(jnp.float32)).astype(jnp.bfloat16)


def mode_factors():
    lane = lax.broadcasted_iota(jnp.int32, (HALF, 128), 1)
    row = lax.broadcasted_iota(jnp.int32, (HALF, 128), 0)
    wave_n = lax.rem(lane, HALF)
    k_x = two_pi * row.astype(jnp.float32)
    k_y = two_pi * wave_n.astype(jnp.float32)
    square = k_x * k_x + k_y * k_y
    keep = jnp.logical_or(row > 0, wave_n > 0)
    safe = jnp.where(keep, square, 1.0)
    damping = jnp.where(keep, jnp.exp(safe * (-1.0 / (6.25 * CELLS * CELLS))) / safe, 0.0)
    images = jnp.where(row > 0, 2.0, 1.0) * jnp.where(wave_n > 0, 2.0, 1.0)
    damping = damping * images
    for_u = damping * k_y * jnp.where(lax.rem(lane, 64) < HALF, 1.0, -1.0)
    for_v = damping * k_x * jnp.where(lane < 64, 1.0, -1.0)
    return for_u, for_v


def halo_box(dr, dc):
    src_rows = {-1: (1, 1), 0: (1, ROWS), 1: (ROWS, 1)}[dr]
    src_cols = {-1: (1, 1), 0: (1, COLS), 1: (COLS, 1)}[dc]
    dst_rows = {-1: (ROWS + 1, 1), 0: (1, ROWS), 1: (0, 1)}[dr]
    dst_cols = {-1: (COLS + 1, 1), 0: (1, COLS), 1: (0, 1)}[dc]
    return tuple(pl.ds(*a) for a in (src_rows, src_cols, dst_rows, dst_cols))


def near_targets(row, col):
    return [
        r * COLS + c
        for r in range(ROWS)
        for c in range(COLS)
        if abs(row - 1 - r) <= 1 and abs(col - 1 - c) <= 1
    ]


def add_near(sources, target, total, cells):
    used = sorted({t for cell in cells for t in cell[3]})
    target_x = {t: jnp.broadcast_to(target[t : t + 1, :], (8, SLOTS)) for t in used}
    target_y = {t: jnp.broadcast_to(target[TILE + t : TILE + t + 1, :], (8, SLOTS)) for t in used}

    at_once = 4 if sum(len(cell[3]) for cell in cells) > 20 else 8

    def groups(step, sums):
        sums = list(sums)
        for part in range(at_once):
            first = pl.multiple_of((step * at_once + part) * 8, 8)
            block = sources[pl.ds(first, 8), :]
            for at_x, at_y, at_s, targets in cells:
                source_x, source_y, strength = (
                    jnp.broadcast_to(block[:, at : at + 1], (8, SLOTS)) for at in (at_x, at_y, at_s)
                )
                for t in targets:
                    a = target_x[t] - source_x
                    b = target_y[t] - source_y
                    q = a * a + b * b
                    w = strength / (jnp.exp2(q) * (q + smooth * alpha))
                    sums[2 * t] = sums[2 * t] - b * w
                    sums[2 * t + 1] = sums[2 * t + 1] + a * w
        return tuple(sums)

    steps = SLOTS // 8 // at_once
    sums = lax.fori_loop(0, steps, groups, tuple(total[k] for k in range(2 * TILE)))
    for k in range(2 * TILE):
        total[k] = sums[k]


def kernel(
    off_hbm, circ_hbm, counts_hbm, field_out,
    off, circ, counts, ext, own_rows, own_t, halo_rows, halo_t, total, near_uv, tab_x, tab_y, sided,
    factors, part, gathered, spread, final,
    halo_send, halo_recv, part_send, part_recv, spread_send, spread_recv, down_send, down_recv, load,
    go,
):
    tx, ty = lax.axis_index("tx"), lax.axis_index("ty")
    x, y, z, c = fan(tx, ty)
    in_plane = z == 0
    is_root = jnp.logical_and(in_plane, c == 1)
    is_guest = jnp.logical_and(jnp.logical_and(x == 0, y == 0), z == 1)
    listens = jnp.logical_or(in_plane, is_guest)

    def host_row(row):
        return jnp.where(jnp.logical_or(row == 3, row == 5), 4, row)

    is_host = jnp.logical_and(jnp.logical_and(in_plane, c == 0), host_row(y) == y)
    loads = [
        pltpu.make_async_copy(src, dst, load.at[k])
        for k, (src, dst) in enumerate(((counts_hbm, counts), (off_hbm, off), (circ_hbm, circ)))
    ]
    for started in loads:
        started.start()
    barrier = pltpu.get_barrier_semaphore()

    def greet(device):
        pl.semaphore_signal(barrier, inc=1, device_id=device, device_id_type=MESH)

    def copy(src, dst, send, recv, device):
        return pltpu.make_async_remote_copy(
            src_ref=src, dst_ref=dst, send_sem=send, recv_sem=recv,
            device_id=device, device_id_type=MESH,
        )

    neighbours = [
        (lax.rem(tx + (TX + dr), TX), lax.rem(ty + (TY + dc), TY)) for dr, dc in directions
    ]
    for k, (n_tx, n_ty) in enumerate(neighbours):
        n_x, n_y, _, _ = fan(n_tx, n_ty)
        host = mesh_id(n_x, host_row(n_y), 0, 0)
        if directions[k] in ((-1, 0), (1, 0)):
            itself = jnp.logical_and(is_host, y == 4) if directions[k] == (-1, 0) else is_host

            @pl.when(jnp.logical_not(itself))
            def _(host=host):
                greet(host)
        else:
            greet(host)

    own_slot = (y * NZ + z) * 2 + c

    @pl.when(listens)
    def _():
        def to_roots(k, carry):
            greet(mesh_id(lax.rem(x + 1 + lax.div(k, NY), NX), lax.rem(y + k, NY), 0, 1))
            return carry

        lax.fori_loop(0, (NX - 1) * NY, to_roots, 0)

    @pl.when(is_root)
    def _():
        def to_column(k, carry):
            slot = lax.rem(own_slot + k, 2 * NY * NZ)
            greet(
                mesh_id(x, lax.div(slot, 2 * NZ), lax.rem(lax.div(slot, 2), NZ), lax.rem(slot, 2))
            )
            return carry

        lax.fori_loop(1, 2 * NY * NZ, to_column, 0)

    for started in loads:
        started.wait()
    row_of = lax.broadcasted_iota(jnp.int32, (TILE, SLOTS), 0)
    lane_of = lax.broadcasted_iota(jnp.int32, (TILE, SLOTS), 1)
    count = jnp.zeros((TILE, SLOTS), jnp.int32)
    for cell in range(TILE):
        count = jnp.where(row_of == cell, counts[cell // COLS, cell % COLS], count)
    live = lane_of < count
    off_x, off_y = off[0], off[1]
    strength = jnp.where(live, circ[...], 0.0)
    cell_row = lax.div(row_of, COLS).astype(jnp.float32)
    cell_col = lax.rem(row_of, COLS).astype(jnp.float32)
    own_rows[2 * TILE : 3 * TILE, :] = strength

    first_col = (ty * COLS).astype(jnp.float32)
    first_row = (tx * ROWS).astype(jnp.float32)
    for cell in range(TILE):
        lanes = slice(cell * SLOTS, (cell + 1) * SLOTS)
        pos_x = (off[0, cell : cell + 1, :] + (first_col + cell % COLS)) * (1.0 / CELLS)
        pos_y = (off[1, cell : cell + 1, :] + (first_row + cell // COLS)) * (1.0 / CELLS)
        weight = own_rows[2 * TILE + cell : 2 * TILE + cell + 1, :]
        for at, table in enumerate(wave_tables(pos_x)):
            rows = slice(at * HALF, (at + 1) * HALF)
            tab_x[rows, lanes] = table
            high, low = split(table * weight)
            sided[rows, lanes] = high
            sided[64 + at * HALF : 64 + (at + 1) * HALF, lanes] = low
        for at, table in enumerate(wave_tables(pos_y)):
            high, low = split(table)
            tab_y[at * HALF : (at + 1) * HALF, lanes] = high
            tab_y[64 + at * HALF : 64 + (at + 1) * HALF, lanes] = high
            tab_y[128 + at * HALF : 128 + (at + 1) * HALF, lanes] = low
    sums = lax.dot_general(
        sided[...], tab_y[64:192, :], (((1,), (1,)), ((), ())),
        preferred_element_type=jnp.float32,
    )
    sums = sums[0:64] + sums[64:128]
    sums = sums + pltpu.roll(sums, 64, 1)
    wide = lax.broadcasted_iota(jnp.int32, (HALF, 128), 1)
    packed = jnp.where(wide < 64, sums[0:HALF], sums[HALF:64])
    for k in range(NY):
        part[k] = packed[4 * k : 4 * k + 4]
    for cell in range(TILE):
        ext[1 + cell // COLS, 1 + cell % COLS, 0] = off[0, cell : cell + 1, :]
        ext[1 + cell // COLS, 1 + cell % COLS, 1] = off[1, cell : cell + 1, :]
        ext[1 + cell // COLS, 1 + cell % COLS, 2] = own_rows[
            2 * TILE + cell : 2 * TILE + cell + 1, :
        ]

    @pl.when(is_root)
    def _():
        pl.semaphore_wait(barrier, (NY - 1) + 2 * NY * (NX - 1) + jnp.where(x == 0, 0, 2))

    def part_copy(k):
        at = lax.rem(y + k, NY)
        return copy(
            part.at[at], gathered.at[own_slot], part_send.at[k], part_recv, mesh_id(x, at, 0, 1)
        )

    def send_parts():
        for k in (4, 3, 5, 2, 6, 1, 7):
            part_copy(k).start()

    @pl.when(is_root)
    def _():
        send_parts()

    @pl.when(jnp.logical_not(jnp.logical_or(is_root, is_host)))
    def _():
        pl.semaphore_wait(barrier, NY)
        send_parts()
        part_copy(0).start()

    field_out[2:4] = off[...]
    field_out[4] = jnp.where(live, 1.0, 0.0)
    own_rows[0:TILE, :] = (off_x + cell_col) * sigma
    own_rows[TILE : 2 * TILE, :] = (off_y + cell_row) * sigma
    own_t[...] = jnp.transpose(own_rows[...])
    total[...] = jnp.zeros_like(total)
    for_u, for_v = mode_factors()
    factors[0] = for_u
    factors[1] = for_v
    add_near(
        own_t, own_rows, total,
        [
            (k, TILE + k, 2 * TILE + k, near_targets(1 + k // COLS, 1 + k % COLS))
            for k in range(TILE)
        ],
    )

    def tell(device):
        pl.semaphore_signal(go, inc=1, device_id=device, device_id_type=MESH)

    @pl.when(is_host)
    def _():
        one_column = 2 * NZ * 8 - 1
        pl.semaphore_wait(barrier, NY + jnp.where(y == 4, 3 * one_column + 1, one_column))
        send_parts()
        part_copy(0).start()
        for k in range(1, 2 * NZ):
            tell(mesh_id(x, y, k // 2, k % 2))

        @pl.when(y == 4)
        def _():
            for k in range(2 * NZ):
                for row in (3, 5):
                    tell(mesh_id(x, row, k // 2, k % 2))

    @pl.when(jnp.logical_not(is_host))
    def _():
        pl.semaphore_wait(go, 1)

    halo = []
    for k, (dr, dc) in enumerate(directions):
        src_rows, src_cols, dst_rows, dst_cols = halo_box(dr, dc)
        halo.append(
            copy(
                ext.at[src_rows, src_cols], ext.at[dst_rows, dst_cols],
                halo_send.at[k], halo_recv.at[k], neighbours[k],
            )
        )
        halo[-1].start()

    def spread_copy(to_x, to_y, to_c):
        return copy(
            spread.at[y * NX + x], spread.at[y * NX + x],
            spread_send.at[to_y, 2 * to_x + to_c], spread_recv, mesh_id(to_x, to_y, 0, to_c),
        )

    def each_spread(act):
        for at, (to_x, to_y, to_c) in enumerate(SPREAD_ORDER):
            if at == 2:
                for core in range(2):
                    act(
                        copy(
                            spread.at[y * NX + x], spread.at[y * NX + x],
                            spread_send.at[NY, core], spread_recv, mesh_id(0, 0, 1, core),
                        )
                    )
            if to_c == 0:
                act(spread_copy(to_x, to_y, to_c))
            else:

                @pl.when(jnp.logical_or(x != to_x, y != to_y))
                def _(to_x=to_x, to_y=to_y, to_c=to_c):
                    act(spread_copy(to_x, to_y, to_c))

    @pl.when(is_root)
    def _():
        gathered[own_slot] = part[y]
        others = pl.ds(0, 2 * NY * NZ - 1)
        pltpu.make_async_copy(gathered.at[others], gathered.at[others], part_recv).wait()
        some = [gathered[k : k + 16] for k in range(0, 2 * NY * NZ, 16)]
        while len(some) > 1:
            some = [some[k] + some[k + 1] for k in range(0, len(some), 2)]
        whole = some[0]
        while whole.shape[0] > 1:
            half = whole.shape[0] // 2
            whole = whole[:half] + whole[half:]
        spread[y * NX + x] = whole[0]
        each_spread(lambda sent: sent.start())

    border = [
        (r, q) for r in range(ROWS + 2) for q in range(COLS + 2)
        if r in (0, ROWS + 1) or q in (0, COLS + 1)
    ]
    for side in (0, 1, -1):
        for k, (dr, dc) in enumerate(directions):
            if dc == -side:
                halo[k].wait_recv()
        cells = [
            (r, q) for r, q in border if (q > COLS) - (q < 1) == side
        ]
        base = {0: 0, 1: 24, -1: 36}[side]
        n = len(cells)
        for k, (r, q) in enumerate(cells):
            halo_rows[base + k : base + k + 1, :] = (ext[r, q, 0] + (q - 1.0)) * sigma
            halo_rows[base + n + k : base + n + k + 1, :] = (ext[r, q, 1] + (r - 1.0)) * sigma
            halo_rows[base + 2 * n + k : base + 2 * n + k + 1, :] = ext[r, q, 2]
        rows = slice({0: 0, 1: 24, -1: 32}[side], {0: 24, 1: 40, -1: 48}[side])
        halo_t[:, rows] = jnp.transpose(halo_rows[rows, :])
        add_near(
            halo_t, own_rows, total,
            [
                (base + k, base + n + k, base + 2 * n + k, near_targets(r, q))
                for k, (r, q) in enumerate(cells)
            ],
        )
    for t in range(TILE):
        for i in range(2):
            near_uv[i, t : t + 1, :] = jnp.sum(total[2 * t + i], axis=0, keepdims=True) * near_scale

    def down_copy(k, at_y=y, core=c):
        return copy(final, final, down_send.at[k], down_recv, mesh_id(x, at_y, k % NZ, core))

    first_chip = jnp.logical_and(x == 0, y == 0)
    stands_in = jnp.logical_and(first_chip, c == 0)

    @pl.when(is_root)
    def _():
        others = pl.ds(0, NX * NY - 1)
        pltpu.make_async_copy(spread.at[others], spread.at[others], spread_recv).wait()

    @pl.when(jnp.logical_and(listens, jnp.logical_not(is_root)))
    def _():
        pltpu.make_async_copy(spread, spread, spread_recv).wait()

    @pl.when(listens)
    def _():
        for k in range(NY):
            final[k] = jnp.sum(spread[k * NX : (k + 1) * NX], axis=0)

    @pl.when(in_plane)
    def _():
        @pl.when(stands_in)
        def _():
            for k in (2, 7):
                down_copy(k + NZ, 0, 1).start()
                down_copy(k).start()

        @pl.when(jnp.logical_not(first_chip))
        def _():
            for k in (1, 7, 2):
                down_copy(k).start()

        @pl.when(y != 0)
        def _():
            for k in (3, 4, 5, 6):
                down_copy(k).start()

        @pl.when(y == NY - 1)
        def _():
            for k in (3, 4, 5, 6):
                down_copy(k + NZ, 0).start()

    @pl.when(jnp.logical_not(listens))
    def _():
        down_copy(1).wait_recv()

    modes = jnp.concatenate([final[k] for k in range(NY)], axis=0)
    swapped = jnp.where(
        lax.rem(wide, 64) < HALF, pltpu.roll(modes, 96, 1), pltpu.roll(modes, 32, 1)
    )
    low_lanes = wide < 64

    def halves(value):
        high = value.astype(jnp.bfloat16).astype(jnp.float32)
        low = value - high
        high_r, low_r = pltpu.roll(high, 64, 1), pltpu.roll(low, 64, 1)
        first = (jnp.where(low_lanes, high, low_r), high)
        second = (jnp.where(low_lanes, high_r, low), high_r)
        return first, second

    u_cos, u_sin = halves(swapped * factors[0])
    v_sin, v_cos = halves(modes * factors[1])
    wide_part = jnp.concatenate([u_cos[0], u_sin[0], v_cos[0], v_sin[0]], axis=0)
    high_part = jnp.concatenate([u_cos[1], u_sin[1], v_cos[1], v_sin[1]], axis=0)
    left = jnp.concatenate(
        [wide_part.astype(jnp.bfloat16), high_part[:, 0:64].astype(jnp.bfloat16)], axis=1
    )
    field = jnp.dot(left, tab_y[...], preferred_element_type=jnp.float32)
    for i in range(2):
        for cell in range(TILE):
            lanes = slice(cell * SLOTS, (cell + 1) * SLOTS)
            product = field[64 * i : 64 * (i + 1), lanes] * tab_x[:, lanes]
            near_uv[i, cell : cell + 1, :] = near_uv[i, cell : cell + 1, :] + jnp.sum(
                product, axis=0, keepdims=True
            )
        field_out[i] = near_uv[i]

    for sent in halo:
        sent.wait_send()
    for k in range(1, NY):
        part_copy(k).wait_send()

    @pl.when(jnp.logical_not(is_root))
    def _():
        part_copy(0).wait_send()

    @pl.when(is_root)
    def _():
        each_spread(lambda sent: sent.wait_send())

    @pl.when(in_plane)
    def _():
        @pl.when(jnp.logical_not(first_chip))
        def _():
            for k in (1, 7, 2):
                down_copy(k).wait_send()

        @pl.when(stands_in)
        def _():
            for k in (2, 7):
                down_copy(k + NZ, 0, 1).wait_send()
                down_copy(k).wait_send()

        @pl.when(y != 0)
        def _():
            for k in (3, 4, 5, 6):
                down_copy(k).wait_send()

        @pl.when(y == NY - 1)
        def _():
            for k in (3, 4, 5, 6):
                down_copy(k + NZ, 0).wait_send()


def per_device(offsets, circ, counts):
    shape = jax.ShapeDtypeStruct((5, TILE, SLOTS), jnp.float32)
    vmem = pl.BlockSpec(memory_space=pltpu.VMEM)
    f32, dma = jnp.float32, pltpu.SemaphoreType.DMA
    hbm = pl.BlockSpec(memory_space=pltpu.HBM)
    field = pl.pallas_call(
        kernel,
        out_shape=shape,
        in_specs=[hbm, hbm, hbm],
        out_specs=vmem,
        scratch_shapes=[
            pltpu.VMEM((2, TILE, SLOTS), f32),
            pltpu.VMEM((TILE, SLOTS), f32),
            pltpu.SMEM((ROWS, COLS), jnp.int32),
            pltpu.VMEM((ROWS + 2, COLS + 2, 3, 1, SLOTS), f32),
            pltpu.VMEM((3 * TILE, SLOTS), f32),
            pltpu.VMEM((SLOTS, 3 * TILE), f32),
            pltpu.VMEM((48, SLOTS), f32),
            pltpu.VMEM((SLOTS, 48), f32),
            pltpu.VMEM((2 * TILE, 8, SLOTS), f32),
            pltpu.VMEM((2, TILE, SLOTS), f32),
            pltpu.VMEM((64, TILE * SLOTS), f32),
            pltpu.VMEM((192, TILE * SLOTS), jnp.bfloat16),
            pltpu.VMEM((128, TILE * SLOTS), jnp.bfloat16),
            pltpu.VMEM((2, HALF, 128), f32),
            pltpu.VMEM((NY, 4, 128), f32),
            pltpu.VMEM((2 * NY * NZ, 4, 128), f32),
            pltpu.VMEM((NY * NX, 4, 128), f32),
            pltpu.VMEM((NY, 4, 128), f32),
            dma((8,)), dma((8,)), dma((NY,)), dma, dma((NY + 1, 2 * NX)), dma, dma((2 * NZ,)), dma,
            dma((3,)), pltpu.SemaphoreType.REGULAR,
        ],
        compiler_params=pltpu.CompilerParams(
            collective_id=0, has_side_effects=True, vmem_limit_bytes=16 << 20
        ),
    )(
        *(
            pltpu.with_memory_space_constraint(value, pltpu.HBM)
            for value in (offsets.reshape(2, TILE, SLOTS), circ.reshape(TILE, SLOTS), counts)
        )
    )
    field = field.reshape((5,) + circ.shape)
    velocity = jnp.where(field[4:5] > 0.0, field[0:2], 0.0)
    return velocity, field[2:4] + section_step * velocity


def solution(mesh):
    spec = P(None, "tx", "ty", None)
    return jax.shard_map(
        per_device,
        mesh=mesh,
        in_specs=(spec, P("tx", "ty", None), P("tx", "ty")),
        out_specs=(spec, spec),
        check_vma=False,
    )
```
